256 devices in a mesh: dp: 8 (over x, core), seq: 32 (over z, y).
Axes of the slice: x: 4, y: 4, z: 8, core: 2. Of those that a mesh axis runs over, the one named last changes fastest.
Arguments:
- queries: bfloat16 [8, 8192, 2048], P('dp', 'seq'), may hold values from -40 to 40
- keys: bfloat16 [8, 8192, 2048], P('dp', 'seq'), may hold values from -40 to 40
- values: bfloat16 [8, 8192, 2048], P('dp', 'seq'), may hold values from -6 to 6
- key_gain: float32 [2048], replicated, may hold values from 0.25 to 1.75
- random_blocks: int32 [16, 128, 3], P(None, 'seq'), may hold values from 2 to 127, as said below
- out_grad: bfloat16 [8, 8192, 2048], P('dp', 'seq'), may hold values from -6 to 6
Outputs:
- attended: bfloat16 [8, 8192, 2048], P('dp', 'seq')
- query_grad: bfloat16 [8, 8192, 2048], P('dp', 'seq')
- key_grad: bfloat16 [8, 8192, 2048], P('dp', 'seq')
- value_grad: bfloat16 [8, 8192, 2048], P('dp', 'seq')
- gain_grad: float32 [2048], replicated
The draws below stay inside these ranges and needn't reach their ends.
Inputs may be any that keep to these rules, and one draw needn't show every extreme that they name: `random_blocks`: for the 4 query blocks of one device, all heads and entries together, at most 9 entries name blocks held by any one device (blocks d * 4 to d * 4 + 3), and exactly 9 name the blocks of some device.
All inputs are finite; a program needn't handle non-finite values.
Results may differ from the reference program's by a relative error of at most 0.03.
The reference program's roundings to bfloat16 on the way count: a program that leaves them out, or rounds other values in their place, can miss the bound.
Values may be sent and summed in bfloat16 or wider, within the bound.
No kernel may reach another device: no remote copies, remote signals or barrier semaphores. Data moves between devices by JAX's collectives and lax.ppermute only.
A program may use at most 128 MiB of HBM per device.

```python
import jax
import jax.numpy as jnp
from jax import lax

HEADS = 16
HD = 128
BLOCK = 64
NG = 2
NR = 3
BATCH = 8
SEQLEN = 8192
BPD = 4
NB = 128
CAP = 9


def base_keys(key):
    raw_keys = jnp.clip(jax.random.normal(jax.random.fold_in(key, 7), (BATCH, SEQLEN, HEADS * HD), jnp.float32), -6.0, 6.0)
    return raw_keys


def draw_keys(key, part):
    return base_keys(key).astype(jnp.bfloat16)


def draw_queries(key, part):
    raw_queries = jnp.clip(jax.random.normal(jax.random.fold_in(key, 13), (BATCH, SEQLEN, HEADS * HD), jnp.float32), -6.0, 6.0)
    return raw_queries.astype(jnp.bfloat16)


def draw_random_blocks(key, part):
    owners = NB // BPD
    request_count = HEADS * BPD * NR

    def one_device(device_index):
        device_key = jax.random.fold_in(key, device_index)
        hottest = jax.random.randint(jax.random.fold_in(device_key, 1), (), 0, owners)
        ordering = jax.random.permutation(jax.random.fold_in(device_key, 2), request_count)
        owner_dev = jnp.where(ordering < CAP, hottest, (hottest + 1 + (ordering - CAP) % (owners - 1)) % owners)
        lowest = jnp.where(owner_dev == 0, NG, 0)
        local_block = jax.random.randint(jax.random.fold_in(device_key, 3), (request_count,), lowest, BPD)
        return (owner_dev * BPD + local_block).astype(jnp.int32)
    table = jax.vmap(one_device)(jnp.arange(owners))
    table = table.reshape(owners, HEADS, BPD, NR).transpose(1, 0, 2, 3).reshape(HEADS, NB, NR)
    return table.astype(jnp.int32)


def block_levels(rng, shape, pieces, low, top_value):
    loudness = 1.0
    for axis_at, parts in pieces:
        draws = jax.random.uniform(jax.random.fold_in(jax.random.fold_in(rng, 6), axis_at), (parts,), jnp.float32, low / len(pieces), top_value / len(pieces))
        loudness = loudness * jnp.repeat(jnp.exp(draws), shape[axis_at] // parts).reshape((-1,) + (1,) * (len(shape) - 1 - axis_at))
    return loudness


def centred(rng, dims, width, limit, split=(), held_as=jnp.bfloat16):
    values = jax.random.normal(rng, dims, jnp.float32) * width
    if len(split) > 0:
        values = block_levels(rng, dims, split, -0.22, 0.18) * values
    return jnp.clip(values, min=-limit, max=limit).astype(held_as)


def setup_inputs(seed: int = 0) -> dict:
    arg_keys = jax.random.split(jax.random.key(seed), 7)
    return {
        "queries": draw_queries(jax.random.fold_in(arg_keys[6], 71), 0),
        "keys": draw_keys(jax.random.fold_in(arg_keys[6], 71), 0),
        "values": centred(arg_keys[2], (BATCH, SEQLEN, HEADS * HD), 1.0, 6.0, ((0, 8), (1, 32))),
        "key_gain": jnp.clip(1.0 + 0.15 * jax.random.normal(arg_keys[3], (HEADS * HD,), jnp.float32), 0.25, 1.75),
        "random_blocks": draw_random_blocks(jax.random.fold_in(arg_keys[6], 71), 0),
        "out_grad": centred(arg_keys[5], (BATCH, SEQLEN, HEADS * HD), 1.0, 6.0, ((0, 8), (1, 32))),
    }


NEGATIVE = -1e30


def rounded(values_in):
    return lax.optimization_barrier(values_in.astype(jnp.bfloat16)).astype(jnp.float32)


def one_head(query_rows, key_rows, value_rows, grad_rows, table):
    score_scale = HD ** -0.5
    query_blocks = query_rows.astype(jnp.float32).reshape(NB, BLOCK, HD)
    key_blocks = key_rows.astype(jnp.float32).reshape(NB, BLOCK, HD)
    value_blocks = value_rows.astype(jnp.float32).reshape(NB, BLOCK, HD)
    grad_blocks = grad_rows.astype(jnp.float32).reshape(NB, BLOCK, HD)
    row_blocks = jnp.arange(NG, NB, dtype=jnp.int32)
    window = row_blocks[:, None] + jnp.arange(-1, 2, dtype=jnp.int32)[None, :]
    global_list = jnp.broadcast_to(jnp.arange(NG, dtype=jnp.int32)[None, :], (NB - NG, NG))
    listing = jnp.concatenate([global_list, window, table[NG:].astype(jnp.int32)], axis=1)
    valid_keys = jnp.concatenate([jnp.ones((NB - NG, NG), bool), (window >= NG) & (window < NB), jnp.ones((NB - NG, NR), bool)], axis=1)
    safe_index = jnp.clip(listing, 0, NB - 1).astype(jnp.int32)
    key_list = key_blocks[safe_index]
    value_list = value_blocks[safe_index]
    query_sel = query_blocks[NG:]
    grad_sel = grad_blocks[NG:]
    key_mask = valid_keys[:, None, :, None]
    scores = jnp.einsum("pbd,pkcd->pbkc", query_sel, key_list) * score_scale
    scores = jnp.where(key_mask, scores, NEGATIVE)
    row_top = jnp.max(scores, axis=(2, 3), keepdims=True)
    expo_vals = jnp.where(key_mask, jnp.exp(scores - row_top), 0.0)
    row_total = jnp.sum(expo_vals, axis=(2, 3), keepdims=True)
    numerator = jnp.einsum("pbkc,pkcd->pbd", rounded(expo_vals), value_list)
    sparse_out = numerator / row_total[..., 0]

    edge_count = NG * BLOCK
    edge_scores = jnp.dot(query_rows[:edge_count], key_rows.T, preferred_element_type=jnp.float32) * score_scale
    edge_top = jnp.max(edge_scores, axis=1, keepdims=True)
    edge_expo = jnp.exp(edge_scores - edge_top)
    edge_total = jnp.sum(edge_expo, axis=1, keepdims=True)
    edge_numer = jnp.dot(edge_expo.astype(jnp.bfloat16), value_rows, preferred_element_type=jnp.float32)
    edge_out = edge_numer / edge_total
    attended = jnp.concatenate([edge_out, sparse_out.reshape(-1, HD)], axis=0).astype(jnp.bfloat16)
    attended_wide = lax.optimization_barrier(attended).astype(jnp.float32)
    row_delta = jnp.sum(grad_rows.astype(jnp.float32) * attended_wide, axis=1)

    delta_sel = row_delta.reshape(NB, BLOCK)[NG:]
    weights = expo_vals / row_total
    dprobs = jnp.einsum("pbd,pkcd->pbkc", grad_sel, value_list)
    dscores = rounded(weights * (dprobs - delta_sel[:, :, None, None]) * score_scale)
    dquery_sparse = jnp.einsum("pbkc,pkcd->pbd", dscores, key_list)
    key_part = jnp.einsum("pbkc,pbd->pkcd", dscores, query_sel)
    value_part = jnp.einsum("pbkc,pbd->pkcd", rounded(weights), grad_sel)
    random_start = NG + 3
    key_part = jnp.concatenate([key_part[:, :random_start], rounded(key_part[:, random_start:])], axis=1)
    value_part = jnp.concatenate([value_part[:, :random_start], rounded(value_part[:, random_start:])], axis=1)
    flat_index = safe_index.reshape(-1)
    key_sum = jax.ops.segment_sum(key_part.reshape(-1, BLOCK, HD), flat_index, num_segments=NB)
    value_sum = jax.ops.segment_sum(value_part.reshape(-1, BLOCK, HD), flat_index, num_segments=NB)

    edge_weights = edge_expo / edge_total
    edge_dprobs = jnp.dot(grad_rows[:edge_count], value_rows.T, preferred_element_type=jnp.float32)
    edge_dscores = (edge_weights * (edge_dprobs - row_delta[:edge_count, None]) * score_scale).astype(jnp.bfloat16)
    edge_dquery = jnp.dot(edge_dscores, key_rows, preferred_element_type=jnp.float32)
    edge_dkey = jnp.dot(edge_dscores.T, query_rows[:edge_count], preferred_element_type=jnp.float32)
    edge_dvalue = jnp.dot(edge_weights.astype(jnp.bfloat16).T, grad_rows[:edge_count], preferred_element_type=jnp.float32)
    query_grad = jnp.concatenate([edge_dquery, dquery_sparse.reshape(-1, HD)], axis=0).astype(jnp.bfloat16)
    key_eff_grad = key_sum.reshape(SEQLEN, HD) + edge_dkey
    value_grad = (value_sum.reshape(SEQLEN, HD) + edge_dvalue).astype(jnp.bfloat16)
    return attended, query_grad, key_eff_grad, value_grad


def reference(queries, keys, values, key_gain, random_blocks, out_grad):
    key_eff = (keys.astype(jnp.float32) * key_gain).astype(jnp.bfloat16)

    def heads_first(array_in):
        return array_in.reshape(BATCH, SEQLEN, HEADS, HD).transpose(0, 2, 1, 3).reshape(BATCH * HEADS, SEQLEN, HD)

    def to_rows(array_in):
        return array_in.reshape(BATCH, HEADS, SEQLEN, HD).transpose(0, 2, 1, 3).reshape(BATCH, SEQLEN, HEADS * HD)

    tables = jnp.broadcast_to(random_blocks[None], (BATCH, HEADS, NB, NR)).reshape(BATCH * HEADS, NB, NR)
    results = lax.map(lambda bundle: one_head(bundle[0], bundle[1], bundle[2], bundle[3], bundle[4]),
                      (heads_first(queries), heads_first(key_eff), heads_first(values), heads_first(out_grad), tables))
    attended = to_rows(results[0])
    query_grad = to_rows(results[1])
    key_eff_grad = to_rows(results[2])
    value_grad = to_rows(results[3])
    key_grad = (key_eff_grad * key_gain).astype(jnp.bfloat16)
    gain_grad = jnp.sum(key_eff_grad * keys.astype(jnp.float32), axis=(0, 1))
    return attended, query_grad, key_grad, value_grad, gain_grad
```

```python
import functools
import math

import jax
import jax.numpy as jnp
from jax import lax
from jax.experimental import pallas as pl
from jax.experimental.pallas import tpu as pltpu
from jax.sharding import PartitionSpec as P

HD = 128
BLOCK = 64
NR = 3
NEGATIVE = -1e30
SCALE = HD**-0.5
EXP_SCALE = SCALE * math.log2(math.e)


def nt(a, b):
    return lax.dot_general(a, b, (((1,), (1,)), ((), ())), preferred_element_type=jnp.float32)


def nn(a, b):
    return lax.dot_general(a, b, (((1,), (0,)), ((), ())), preferred_element_type=jnp.float32)


def tn(a, b):
    return lax.dot_general(a, b, (((0,), (0,)), ((), ())), preferred_element_type=jnp.float32)


def pack_kernel(group, a_ref, b_ref, out_ref):
    for h in range(group):
        for slot, ref in enumerate((a_ref, b_ref)):
            for block in range(4):
                out_ref[block % 2, h, slot, block // 2] = ref[
                    block * BLOCK : (block + 1) * BLOCK, h * HD : (h + 1) * HD
                ]


def pack(a, b, heads):
    group = min(heads, 4)
    spec = pl.BlockSpec((4 * BLOCK, group * HD), lambda i: (0, i))
    return pl.pallas_call(
        functools.partial(pack_kernel, group),
        grid=(heads // group,),
        in_specs=[spec, spec],
        out_specs=pl.BlockSpec((2, group, 2, 2, BLOCK, HD), lambda i: (0, i, 0, 0, 0, 0)),
        out_shape=jax.ShapeDtypeStruct((2, heads, 2, 2, BLOCK, HD), a.dtype),
        name="pack",
    )(a, b)


def unpack_kernel(group, in_ref, a_ref, b_ref):
    for h in range(group):
        for slot, ref in enumerate((a_ref, b_ref)):
            for block in range(4):
                ref[block * BLOCK : (block + 1) * BLOCK, h * HD : (h + 1) * HD] = in_ref[
                    block % 2, h, slot, block // 2
                ]


def unpack(x, heads):
    group = min(heads, 4)
    spec = pl.BlockSpec((4 * BLOCK, group * HD), lambda i: (0, i))
    shape = jax.ShapeDtypeStruct((4 * BLOCK, heads * HD), x.dtype)
    return pl.pallas_call(
        functools.partial(unpack_kernel, group),
        grid=(heads // group,),
        in_specs=[pl.BlockSpec((2, group, 2, 2, BLOCK, HD), lambda i: (0, i, 0, 0, 0, 0))],
        out_specs=[spec, spec],
        out_shape=[shape, shape],
        name="unpack",
    )(x)


def attention_kernel(
    places,
    unroll,
    core_ref,
    table_ref,
    gain_ref,
    qg_ref,
    kv_own,
    kv_other,
    ad_ref,
    own_out,
    other_out,
    k_scr,
    v_scr,
    acc_k,
    acc_v,
    score_scr,
    in_sem,
    out_sem,
):
    core = core_ref[0]
    total_blocks = 4 * places
    chunk = 4
    copies = [
        pltpu.make_async_copy(kv_own.at[:, 0], k_scr.at[core], in_sem.at[0]),
        pltpu.make_async_copy(kv_other.at[:, 0], k_scr.at[1 - core], in_sem.at[1]),
        pltpu.make_async_copy(kv_own.at[:, 1], v_scr.at[core], in_sem.at[2]),
        pltpu.make_async_copy(kv_other.at[:, 1], v_scr.at[1 - core], in_sem.at[3]),
    ]
    for copy in copies:
        copy.start()
    for copy in copies:
        copy.wait()

    gain = gain_ref[...]
    for parity in range(2):

        def scale_keys(t, carry):
            rows = k_scr[parity, pl.ds(t * chunk, chunk)].astype(jnp.float32)
            k_scr[parity, pl.ds(t * chunk, chunk)] = (rows * gain).astype(jnp.bfloat16)
            return carry

        lax.fori_loop(0, places // chunk, scale_keys, 0)

    steps = places // chunk
    width = chunk * 2 * BLOCK
    query = qg_ref[0, 0, 0]
    grad = qg_ref[0, 1, 0]

    def lanes(x, op):
        out = x[:, :HD]
        for t in range(1, width // HD):
            out = op(out, x[:, t * HD : (t + 1) * HD])
        return out

    def rows_of(ref, t):
        return ref[t // steps, pl.ds((t % steps) * chunk, chunk)].reshape(width, HD)

    def dense_scores(t, top):
        scores = nt(query, rows_of(k_scr, t))
        score_scr[t] = scores
        return jnp.maximum(top, lanes(scores, jnp.maximum))

    top = lax.fori_loop(
        0, 2 * steps, dense_scores, jnp.full((BLOCK, HD), NEGATIVE, jnp.float32)
    )
    top = jnp.max(top, axis=1, keepdims=True)

    def dense_expo(t, carry):
        total, numer = carry
        expo = jnp.exp2((score_scr[t] - top) * EXP_SCALE)
        score_scr[t] = expo
        numer = numer + nn(expo.astype(jnp.bfloat16), rows_of(v_scr, t))
        return total + lanes(expo, jnp.add), numer

    zero = jnp.zeros((BLOCK, HD), jnp.float32)
    total, numer = lax.fori_loop(0, 2 * steps, dense_expo, (zero, zero))
    inverse = 1.0 / jnp.sum(total, axis=1, keepdims=True)
    attended = (numer * inverse).astype(jnp.bfloat16)
    ad_ref[0, 0, 0] = attended
    delta = jnp.sum(grad.astype(jnp.float32) * attended.astype(jnp.float32), axis=1, keepdims=True)

    def dense_back(t, dquery):
        key_rows = rows_of(k_scr, t)
        weights = score_scr[t] * inverse
        dprobs = nt(grad, rows_of(v_scr, t))
        dscores = (weights * (dprobs - delta) * SCALE).astype(jnp.bfloat16)
        where = (t // steps, pl.ds((t % steps) * chunk, chunk))
        acc_k[where] = tn(dscores, query).reshape(chunk, 2, BLOCK, HD)
        acc_v[where] = tn(weights.astype(jnp.bfloat16), grad).reshape(chunk, 2, BLOCK, HD)
        return dquery + nn(dscores, key_rows)

    dquery = lax.fori_loop(0, 2 * steps, dense_back, zero)
    ad_ref[0, 1, 0] = dquery.astype(jnp.bfloat16)

    column = lax.broadcasted_iota(jnp.int32, (1, 8 * BLOCK), 1) // BLOCK

    def locate(block):
        half = block // 2
        return (block % 2, half // 2, half % 2)

    def sparse_block(n):
        block = 2 * n + core
        at_query = (n // 2, n % 2)
        listing = [
            (0, 0, 0),
            (1, 0, 0),
            locate(jnp.maximum(block - 1, 0)),
            locate(block),
            locate(jnp.minimum(block + 1, total_blocks - 1)),
        ] + [locate(table_ref[n * NR + r]) for r in range(NR)]
        query = qg_ref[at_query[0], 0, at_query[1]]
        grad = qg_ref[at_query[0], 1, at_query[1]]
        key_list = jnp.concatenate([k_scr[where] for where in listing], axis=0)
        value_list = jnp.concatenate([v_scr[where] for where in listing], axis=0)
        masked = ((column == 2) & (block == 2)) | ((column == 4) & (block == total_blocks - 1))
        scores = nt(query, key_list) + jnp.where(masked, NEGATIVE, 0.0)
        top = jnp.max(scores, axis=1, keepdims=True)
        expo = jnp.exp2((scores - top) * EXP_SCALE)
        inverse = 1.0 / jnp.sum(expo, axis=1, keepdims=True)
        numer = nn(expo.astype(jnp.bfloat16), value_list)
        attended = (numer * inverse).astype(jnp.bfloat16)
        delta = jnp.sum(
            grad.astype(jnp.float32) * attended.astype(jnp.float32), axis=1, keepdims=True
        )
        dprobs = nt(grad, value_list)
        weights = expo * inverse
        dscores = (weights * (dprobs - delta) * SCALE).astype(jnp.bfloat16)
        dquery = nn(dscores, key_list)
        dkey = tn(dscores, query)
        dvalue = tn(weights.astype(jnp.bfloat16), grad)
        ad_ref[at_query[0], 0, at_query[1]] = attended
        ad_ref[at_query[0], 1, at_query[1]] = dquery.astype(jnp.bfloat16)
        return listing, dkey, dvalue

    def sparse_step(t, carry):
        done = [sparse_block(1 + t * unroll + u) for u in range(unroll)]
        for listing, dkey, dvalue in done:
            for slot, where in enumerate(listing):
                acc_k[where] += dkey[slot * BLOCK : (slot + 1) * BLOCK]
                acc_v[where] += dvalue[slot * BLOCK : (slot + 1) * BLOCK]
        return carry

    lax.fori_loop(0, (2 * places - 1) // unroll, sparse_step, 0)

    def round_other(t, carry):
        where = pl.ds(t * chunk, chunk)
        other_out[where, 0] = acc_k[1 - core, where].astype(jnp.bfloat16)
        other_out[where, 1] = acc_v[1 - core, where].astype(jnp.bfloat16)
        return carry

    copies = [
        pltpu.make_async_copy(acc_k.at[core], own_out.at[:, 0], out_sem.at[0]),
        pltpu.make_async_copy(acc_v.at[core], own_out.at[:, 1], out_sem.at[1]),
    ]
    for copy in copies:
        copy.start()
    lax.fori_loop(0, places // chunk, round_other, 0)
    for copy in copies:
        copy.wait()


def attention(core, table, gain, qg, kv_own, kv_other, places):
    unroll = 3 if (2 * places - 1) % 3 == 0 else 1
    shape = (places, 2, 2, BLOCK, HD)
    half = (2, places, 2, BLOCK, HD)
    smem = pl.BlockSpec(memory_space=pltpu.SMEM)
    vmem = pl.BlockSpec(memory_space=pltpu.VMEM)
    hbm = pl.BlockSpec(memory_space=pl.ANY)
    return pl.pallas_call(
        functools.partial(attention_kernel, places, unroll),
        in_specs=[smem, smem, vmem, vmem, hbm, hbm],
        out_specs=[vmem, hbm, vmem],
        out_shape=[
            jax.ShapeDtypeStruct(shape, jnp.bfloat16),
            jax.ShapeDtypeStruct(shape, jnp.float32),
            jax.ShapeDtypeStruct(shape, jnp.bfloat16),
        ],
        scratch_shapes=[
            pltpu.VMEM(half, jnp.bfloat16),
            pltpu.VMEM(half, jnp.bfloat16),
            pltpu.VMEM(half, jnp.float32),
            pltpu.VMEM(half, jnp.float32),
            pltpu.VMEM((places // 2, BLOCK, 8 * BLOCK), jnp.float32),
            pltpu.SemaphoreType.DMA((4,)),
            pltpu.SemaphoreType.DMA((2,)),
        ],
        compiler_params=pltpu.CompilerParams(vmem_limit_bytes=48 * 1024 * 1024),
        name="attention",
    )(core, table, gain, qg, kv_own, kv_other)


def finish_kernel(own_ref, other_ref, kv_ref, gain_ref, out_ref, gain_out):
    gain = gain_ref[...]
    dkey = own_ref[:, 0] + other_ref[:, 0].astype(jnp.float32)
    out_ref[:, 0] = (dkey * gain).astype(jnp.bfloat16)
    out_ref[:, 1] = (own_ref[:, 1] + other_ref[:, 1].astype(jnp.float32)).astype(jnp.bfloat16)
    term = jnp.sum(dkey * kv_ref[:, 0].astype(jnp.float32), axis=(0, 1, 2)).reshape(1, HD)

    @pl.when(pl.program_id(0) == 0)
    def _():
        gain_out[...] = term

    @pl.when(pl.program_id(0) > 0)
    def _():
        gain_out[...] += term


def finish(own, other, kv, gain, places):
    group = 4
    block = (group, 2, 2, BLOCK, HD)
    spec = pl.BlockSpec(block, lambda i: (i, 0, 0, 0, 0))
    row = pl.BlockSpec((1, HD), lambda i: (0, 0))
    return pl.pallas_call(
        finish_kernel,
        grid=(places // group,),
        in_specs=[spec, spec, spec, row],
        out_specs=[spec, row],
        out_shape=[
            jax.ShapeDtypeStruct(own.shape, jnp.bfloat16),
            jax.ShapeDtypeStruct((1, HD), jnp.float32),
        ],
        name="finish",
    )(own, other, kv, gain)


def shards(queries, keys, values, key_gain, random_blocks, out_grad):
    heads = queries.shape[2] // HD
    places = lax.axis_size("seq")
    dp = lax.axis_size("dp")
    core = lax.axis_index("dp") % 2
    head = lax.axis_index("seq") % heads
    pairs = [[i, i + 1] for i in range(0, dp, 2)]
    swap = [(i, i ^ 1) for i in range(dp)]

    def between_cores(x):
        return lax.all_to_all(
            x, "dp", split_axis=0, concat_axis=0, axis_index_groups=pairs, tiled=True
        )

    def over_seq(x):
        return lax.all_to_all(x, "seq", split_axis=0, concat_axis=0, tiled=True)

    shape = (places, 2, 2, BLOCK, HD)
    by_parity = (2, heads, 2, 2, BLOCK, HD)

    named = lax.dynamic_index_in_dim(
        random_blocks.reshape(heads, 2, 2, NR), core, axis=2, keepdims=False
    ).reshape(1, heads, 2 * NR)
    table = over_seq(jnp.broadcast_to(named, (2, heads, 2 * NR)).reshape(places, 2 * NR))
    gain = lax.dynamic_slice_in_dim(key_gain, head * HD, HD).reshape(1, HD)

    kv = over_seq(between_cores(pack(keys[0], values[0], heads)).reshape(shape))
    qg = over_seq(between_cores(pack(queries[0], out_grad[0], heads)).reshape(shape))
    kv_other = lax.ppermute(kv, "dp", swap)

    ad, own, other = attention(
        core.reshape(1), table.reshape(2 * places * NR), gain, qg, kv, kv_other, places
    )
    ad = between_cores(over_seq(ad).reshape(by_parity))
    attended, query_grad = unpack(ad, heads)

    dkv, gain_term = finish(own, lax.ppermute(other, "dp", swap), kv, gain, places)
    gain_terms = over_seq(jnp.broadcast_to(gain_term, (places, HD)))
    gain_sum = jnp.sum(gain_terms.reshape(2, heads * HD), axis=0)
    gain_all = lax.all_to_all(
        jnp.broadcast_to(gain_sum, (dp, heads * HD)), "dp", split_axis=0, concat_axis=0, tiled=True
    )
    gain_grad = jnp.sum(gain_all, axis=0)

    dkv = between_cores(over_seq(dkv).reshape(by_parity))
    key_grad, value_grad = unpack(dkv, heads)
    return (attended[None], query_grad[None], key_grad[None], value_grad[None], gain_grad)


def solution(mesh):
    rows = P("dp", "seq", None)
    return jax.shard_map(
        shards,
        mesh=mesh,
        in_specs=(rows, rows, rows, P(), P(None, "seq", None), rows),
        out_specs=(rows, rows, rows, rows, P()),
        check_vma=False,
    )
```

```python
import functools
import math

import jax
import jax.numpy as jnp
from jax import lax
from jax.experimental import pallas as pl
from jax.experimental.pallas import tpu as pltpu
from jax.sharding import PartitionSpec as P

HD = 128
BLOCK = 64
NR = 3
NK = 8
PAIR = 2 * BLOCK
CHUNK = 4
WIDTH = CHUNK * PAIR
SPARE = 16
NEGATIVE = -1e30
SCALE = HD**-0.5
EXP_SCALE = SCALE * math.log2(math.e)
VMEM_LIMIT = 56 * 1024 * 1024


def nt(a, b):
    return lax.dot_general(a, b, (((1,), (1,)), ((), ())), preferred_element_type=jnp.float32)


def nn(a, b):
    return lax.dot_general(a, b, (((1,), (0,)), ((), ())), preferred_element_type=jnp.float32)


def tn(a, b):
    return lax.dot_general(a, b, (((0,), (0,)), ((), ())), preferred_element_type=jnp.float32)


def pack_kernel(group, count, with_spare, core_ref, *refs):
    core = core_ref[0]
    keep_ref, send_ref = refs[-2:]
    for out_ref, parity in ((keep_ref, core), (send_ref, 1 - core)):
        for h in range(group):
            columns = slice(h * HD, (h + 1) * HD)
            for slot in range(count):
                for turn in range(2):
                    row = slot * PAIR + turn * BLOCK
                    at = pl.multiple_of((2 * turn + parity) * BLOCK, BLOCK)
                    out_ref[h, row : row + BLOCK] = refs[slot][pl.ds(at, BLOCK), columns]
            if with_spare:
                out_ref[h, count * PAIR :] = jnp.broadcast_to(
                    refs[count][parity, h], (SPARE, HD)
                )


def pack(core, arrays, spare, heads):
    group = min(heads, 4)
    count = len(arrays)
    rows = count * PAIR + (SPARE if spare is not None else 0)
    specs = [pl.BlockSpec((4 * BLOCK, group * HD), lambda i, c: (0, i))] * count
    args = list(arrays)
    if spare is not None:
        specs.append(pl.BlockSpec((2, group, 1, HD), lambda i, c: (0, i, 0, 0)))
        args.append(spare)
    return pl.pallas_call(
        functools.partial(pack_kernel, group, count, spare is not None),
        grid_spec=pltpu.PrefetchScalarGridSpec(
            num_scalar_prefetch=1,
            grid=(heads // group,),
            in_specs=specs,
            out_specs=[
                pl.BlockSpec((pl.Squeezed(), group, rows, HD), lambda i, c: (c[0], i, 0, 0)),
                pl.BlockSpec((group, rows, HD), lambda i, c: (i, 0, 0)),
            ],
        ),
        out_shape=[
            jax.ShapeDtypeStruct((2, heads, rows, HD), jnp.bfloat16),
            jax.ShapeDtypeStruct((heads, rows, HD), jnp.bfloat16),
        ],
        name="pack",
    )(core, *args)


def unpack_kernel(group, core_ref, keep_ref, came_ref, *out_refs):
    core = core_ref[0]
    for in_ref, parity in ((keep_ref, core), (came_ref, 1 - core)):
        for h in range(group):
            for slot, ref in enumerate(out_refs):
                for turn in range(2):
                    row = slot * PAIR + turn * BLOCK
                    at = pl.multiple_of((2 * turn + parity) * BLOCK, BLOCK)
                    ref[pl.ds(at, BLOCK), h * HD : (h + 1) * HD] = in_ref[h, row : row + BLOCK]


def unpack(core, keep, came, count):
    heads, rows = keep.shape[1:3]
    group = min(heads, 4)
    return pl.pallas_call(
        functools.partial(unpack_kernel, group),
        grid_spec=pltpu.PrefetchScalarGridSpec(
            num_scalar_prefetch=1,
            grid=(heads // group,),
            in_specs=[
                pl.BlockSpec((pl.Squeezed(), group, rows, HD), lambda i, c: (c[0], i, 0, 0)),
                pl.BlockSpec((group, rows, HD), lambda i, c: (i, 0, 0)),
            ],
            out_specs=[pl.BlockSpec((4 * BLOCK, group * HD), lambda i, c: (0, i))] * count,
        ),
        out_shape=[jax.ShapeDtypeStruct((4 * BLOCK, heads * HD), keep.dtype)] * count,
        name="unpack",
    )(core, keep, came)


def locate(block):
    half = block // 2
    return (block % 2, half // 2, pl.ds(pl.multiple_of((half % 2) * BLOCK, BLOCK), BLOCK))


def key_places(table_ref, n, block, total_blocks):
    return [
        (0, 0, pl.ds(0, BLOCK)),
        (1, 0, pl.ds(0, BLOCK)),
        locate(jnp.maximum(block - 1, 0)),
        locate(block),
        locate(jnp.minimum(block + 1, total_blocks - 1)),
    ] + [locate(table_ref[n * NR + r]) for r in range(NR)]


def chunk_rows(ref, t, steps):
    return ref[t // steps, pl.ds((t % steps) * CHUNK, CHUNK)].reshape(WIDTH, HD)


def forward_kernel(
    places,
    unroll,
    core_ref,
    table_ref,
    gain_ref,
    own_ref,
    other_ref,
    att_ref,
    weight_ref,
    dense_ref,
    key_out,
    k_scr,
    v_scr,
    q_scr,
    score_scr,
    in_sem,
    out_sem,
):
    core = core_ref[0]
    total_blocks = 4 * places
    steps = places // CHUNK

    def rows(ref, slot):
        return ref.at[:, slot * PAIR : (slot + 1) * PAIR]

    copies = [
        pltpu.make_async_copy(rows(own_ref, 0), k_scr.at[core], in_sem.at[0]),
        pltpu.make_async_copy(rows(other_ref, 0), k_scr.at[1 - core], in_sem.at[1]),
        pltpu.make_async_copy(rows(own_ref, 2), q_scr, in_sem.at[2]),
        pltpu.make_async_copy(rows(own_ref, 1), v_scr.at[core], in_sem.at[3]),
        pltpu.make_async_copy(rows(other_ref, 1), v_scr.at[1 - core], in_sem.at[4]),
    ]
    for copy in copies:
        copy.start()
    for copy in copies[:3]:
        copy.wait()

    gain = gain_ref[...]
    query = q_scr[0, :BLOCK]

    def lanes(x, op):
        out = x[:, :HD]
        for t in range(1, WIDTH // HD):
            out = op(out, x[:, t * HD : (t + 1) * HD])
        return out

    def dense_scores(t, top):
        where = (t // steps, pl.ds((t % steps) * CHUNK, CHUNK))
        keys = (k_scr[where].astype(jnp.float32) * gain).astype(jnp.bfloat16)
        k_scr[where] = keys
        scores = nt(query, keys.reshape(WIDTH, HD))
        score_scr[t] = scores
        return jnp.maximum(top, lanes(scores, jnp.maximum))

    top = lax.fori_loop(
        0, 2 * steps, dense_scores, jnp.full((BLOCK, HD), NEGATIVE, jnp.float32)
    )
    top = jnp.max(top, axis=1, keepdims=True)
    key_copy = pltpu.make_async_copy(k_scr, key_out, out_sem)
    key_copy.start()
    for copy in copies[3:]:
        copy.wait()

    def dense_expo(t, carry):
        total, numer = carry
        expo = jnp.exp2((score_scr[t] - top) * EXP_SCALE)
        score_scr[t] = expo
        numer = numer + nn(expo.astype(jnp.bfloat16), chunk_rows(v_scr, t, steps))
        return total + lanes(expo, jnp.add), numer

    zero = jnp.zeros((BLOCK, HD), jnp.float32)
    total, numer = lax.fori_loop(0, 2 * steps, dense_expo, (zero, zero))
    inverse = 1.0 / jnp.sum(total, axis=1, keepdims=True)
    att_ref[0, :BLOCK] = (numer * inverse).astype(jnp.bfloat16)

    def dense_weights(t, carry):
        dense_ref[t] = (score_scr[t] * inverse).astype(jnp.bfloat16)
        return carry

    lax.fori_loop(0, 2 * steps, dense_weights, 0)

    column = lax.broadcasted_iota(jnp.int32, (1, NK * BLOCK), 1) // BLOCK

    def sparse_block(n):
        block = 2 * n + core
        listing = key_places(table_ref, n, block, total_blocks)
        key_list = jnp.concatenate([k_scr[where] for where in listing], axis=0)
        value_list = jnp.concatenate([v_scr[where] for where in listing], axis=0)
        mine = (n // 2, pl.ds(pl.multiple_of((n % 2) * BLOCK, BLOCK), BLOCK))
        masked = ((column == 2) & (block == 2)) | ((column == 4) & (block == total_blocks - 1))
        scores = nt(q_scr[mine], key_list) + jnp.where(masked, NEGATIVE, 0.0)
        top = jnp.max(scores, axis=1, keepdims=True)
        expo = jnp.exp2((scores - top) * EXP_SCALE)
        inverse = 1.0 / jnp.sum(expo, axis=1, keepdims=True)
        numer = nn(expo.astype(jnp.bfloat16), value_list)
        return mine, (numer * inverse).astype(jnp.bfloat16), (expo * inverse).astype(jnp.bfloat16)

    def sparse_step(t, carry):
        first = 1 + t * unroll
        done = [sparse_block(first + u) for u in range(unroll)]
        for u, (mine, attended, weights) in enumerate(done):
            att_ref[mine] = attended
            weight_ref[first + u] = weights
        return carry

    lax.fori_loop(0, (2 * places - 1) // unroll, sparse_step, 0)
    key_copy.wait()


def forward(core, table, gain, own, other, places):
    unroll = 3 if (2 * places - 1) % 3 == 0 else 1
    both = (2, places, PAIR, HD)
    smem = pl.BlockSpec(memory_space=pltpu.SMEM)
    vmem = pl.BlockSpec(memory_space=pltpu.VMEM)
    hbm = pl.BlockSpec(memory_space=pl.ANY)
    blocks = 2 * places
    return pl.pallas_call(
        functools.partial(forward_kernel, places, unroll),
        in_specs=[smem, smem, vmem, hbm, hbm],
        out_specs=[vmem, vmem, vmem, hbm],
        out_shape=[
            jax.ShapeDtypeStruct((places, PAIR, HD), jnp.bfloat16),
            jax.ShapeDtypeStruct((blocks, BLOCK, NK * BLOCK), jnp.bfloat16),
            jax.ShapeDtypeStruct((places // 2, BLOCK, WIDTH), jnp.bfloat16),
            jax.ShapeDtypeStruct(both, jnp.bfloat16),
        ],
        scratch_shapes=[
            pltpu.VMEM(both, jnp.bfloat16),
            pltpu.VMEM(both, jnp.bfloat16),
            pltpu.VMEM((places, PAIR, HD), jnp.bfloat16),
            pltpu.VMEM((places // 2, BLOCK, WIDTH), jnp.float32),
            pltpu.SemaphoreType.DMA((5,)),
            pltpu.SemaphoreType.DMA,
        ],
        compiler_params=pltpu.CompilerParams(vmem_limit_bytes=VMEM_LIMIT),
        cost_estimate=pl.CostEstimate(
            flops=4 * blocks * BLOCK * HD * 3 * NK * BLOCK,
            bytes_accessed=60 << 20,
            transcendentals=blocks * BLOCK * NK * BLOCK,
        ),
        name="forward",
    )(core, table, gain, own, other)


def backward_kernel(
    places,
    unroll,
    core_ref,
    table_ref,
    own_ref,
    other_ref,
    key_ref,
    grad_ref,
    att_ref,
    weight_ref,
    dense_ref,
    dq_ref,
    own_out,
    other_out,
    gain_out,
    k_scr,
    v_scr,
    q_scr,
    g_scr,
    a_scr,
    weight_scr,
    dense_scr,
    acc_k,
    acc_v,
    raw_scr,
    in_sem,
    out_sem,
):
    core = core_ref[0]
    total_blocks = 4 * places
    steps = places // CHUNK

    def rows(ref, slot):
        return ref.at[:, slot * PAIR : (slot + 1) * PAIR]

    copies = [
        pltpu.make_async_copy(src, dst, in_sem.at[at])
        for at, (src, dst) in enumerate(
            [
                (grad_ref, g_scr),
                (att_ref, a_scr),
                (dense_ref, dense_scr),
                (rows(own_ref, 1), v_scr.at[core]),
                (rows(other_ref, 1), v_scr.at[1 - core]),
                (key_ref, k_scr),
                (rows(own_ref, 2), q_scr),
                (weight_ref, weight_scr),
                (rows(own_ref, 0), raw_scr.at[core]),
                (rows(other_ref, 0), raw_scr.at[1 - core]),
            ]
        )
    ]
    for copy in copies:
        copy.start()
    for copy in copies[:7]:
        copy.wait()

    def row_delta(grad, attended):
        return jnp.sum(
            grad.astype(jnp.float32) * attended.astype(jnp.float32), axis=1, keepdims=True
        )

    query = q_scr[0, :BLOCK]
    grad = g_scr[0, :BLOCK]
    delta = row_delta(grad, a_scr[0, :BLOCK])

    def dense_back(t, dquery):
        weights = dense_scr[t]
        dprobs = nt(grad, chunk_rows(v_scr, t, steps))
        dscores = (weights.astype(jnp.float32) * (dprobs - delta)).astype(jnp.bfloat16)
        where = (t // steps, pl.ds((t % steps) * CHUNK, CHUNK))
        acc_k[where] = tn(dscores, query).reshape(CHUNK, PAIR, HD)
        acc_v[where] = tn(weights, grad).reshape(CHUNK, PAIR, HD)
        return dquery + nn(dscores, chunk_rows(k_scr, t, steps))

    dquery = lax.fori_loop(0, 2 * steps, dense_back, jnp.zeros((BLOCK, HD), jnp.float32))
    dq_ref[0, :BLOCK] = (dquery * SCALE).astype(jnp.bfloat16)
    for copy in copies[7:]:
        copy.wait()

    def sparse_block(n):
        block = 2 * n + core
        listing = key_places(table_ref, n, block, total_blocks)
        key_list = jnp.concatenate([k_scr[where] for where in listing], axis=0)
        value_list = jnp.concatenate([v_scr[where] for where in listing], axis=0)
        mine = (n // 2, pl.ds(pl.multiple_of((n % 2) * BLOCK, BLOCK), BLOCK))
        grad = g_scr[mine]
        weights = weight_scr[n]
        delta = row_delta(grad, a_scr[mine])
        dprobs = nt(grad, value_list)
        dscores = (weights.astype(jnp.float32) * (dprobs - delta)).astype(jnp.bfloat16)
        dquery = nn(dscores, key_list)
        dkey = tn(dscores, q_scr[mine])
        dvalue = tn(weights, grad)
        return listing, mine, dquery, dkey, dvalue

    def sparse_step(t, carry):
        done = [sparse_block(1 + t * unroll + u) for u in range(unroll)]
        for listing, mine, dquery, dkey, dvalue in done:
            dq_ref[mine] = (dquery * SCALE).astype(jnp.bfloat16)
            for slot, where in enumerate(listing):
                acc_k[where] += dkey[slot * BLOCK : (slot + 1) * BLOCK]
                acc_v[where] += dvalue[slot * BLOCK : (slot + 1) * BLOCK]
        return carry

    lax.fori_loop(0, (2 * places - 1) // unroll, sparse_step, 0)

    copies = [
        pltpu.make_async_copy(acc_k.at[core], own_out.at[0], out_sem.at[0]),
        pltpu.make_async_copy(acc_v.at[core], own_out.at[1], out_sem.at[1]),
    ]
    for copy in copies:
        copy.start()

    def round_other(t, carry):
        where = pl.ds(t * CHUNK, CHUNK)
        mine = acc_k[core, where] * raw_scr[core, where].astype(jnp.float32)
        far = acc_k[1 - core, where]
        theirs = far * raw_scr[1 - core, where].astype(jnp.float32)
        other_out[0, where] = far.astype(jnp.bfloat16)
        other_out[1, where] = acc_v[1 - core, where].astype(jnp.bfloat16)
        return carry + jnp.sum((mine + theirs).reshape(CHUNK * PAIR // 8, 8, HD), axis=0)

    gain_term = lax.fori_loop(0, steps, round_other, jnp.zeros((8, HD), jnp.float32))
    gain_term = jnp.sum(gain_term, axis=0, keepdims=True) * SCALE
    gain_out[...] = jnp.broadcast_to(gain_term, (8, HD))
    for copy in copies:
        copy.wait()


def backward(core, table, own, other, keys, grads, att, weights, dense, places):
    unroll = 3 if (2 * places - 1) % 3 == 0 else 1
    both = (2, places, PAIR, HD)
    half = (places, PAIR, HD)
    blocks = 2 * places
    smem = pl.BlockSpec(memory_space=pltpu.SMEM)
    vmem = pl.BlockSpec(memory_space=pltpu.VMEM)
    hbm = pl.BlockSpec(memory_space=pl.ANY)
    return pl.pallas_call(
        functools.partial(backward_kernel, places, unroll),
        in_specs=[smem, smem] + [hbm] * 7,
        out_specs=[vmem, hbm, vmem, vmem],
        out_shape=[
            jax.ShapeDtypeStruct(half, jnp.bfloat16),
            jax.ShapeDtypeStruct(both, jnp.float32),
            jax.ShapeDtypeStruct(both, jnp.bfloat16),
            jax.ShapeDtypeStruct((8, HD), jnp.float32),
        ],
        scratch_shapes=[
            pltpu.VMEM(both, jnp.bfloat16),
            pltpu.VMEM(both, jnp.bfloat16),
            pltpu.VMEM(half, jnp.bfloat16),
            pltpu.VMEM(half, jnp.bfloat16),
            pltpu.VMEM(half, jnp.bfloat16),
            pltpu.VMEM(weights.shape, jnp.bfloat16),
            pltpu.VMEM(dense.shape, jnp.bfloat16),
            pltpu.VMEM(both, jnp.float32),
            pltpu.VMEM(both, jnp.float32),
            pltpu.VMEM(both, jnp.bfloat16),
            pltpu.SemaphoreType.DMA((10,)),
            pltpu.SemaphoreType.DMA((2,)),
        ],
        compiler_params=pltpu.CompilerParams(vmem_limit_bytes=VMEM_LIMIT),
        cost_estimate=pl.CostEstimate(
            flops=8 * blocks * BLOCK * HD * 3 * NK * BLOCK,
            bytes_accessed=100 << 20,
            transcendentals=0,
        ),
        name="backward",
    )(core, table, own, other, keys, grads, att, weights, dense)


def finish_kernel(own_ref, other_ref, scaled_gain_ref, gain_grad_ref, out_ref):
    gain = scaled_gain_ref[...]
    dkey = own_ref[0] + other_ref[0].astype(jnp.float32)
    out_ref[:, :PAIR] = (dkey * gain).astype(jnp.bfloat16)
    dvalue = own_ref[1] + other_ref[1].astype(jnp.float32)
    out_ref[:, PAIR : 2 * PAIR] = dvalue.astype(jnp.bfloat16)
    total = gain_grad_ref[...]
    high = total.astype(jnp.bfloat16)
    rest = total - high.astype(jnp.float32)
    middle = rest.astype(jnp.bfloat16)
    low = (rest - middle.astype(jnp.float32)).astype(jnp.bfloat16)
    row = lax.broadcasted_iota(jnp.int32, (SPARE, HD), 0)
    spare = jnp.where(
        row == 0,
        high.astype(jnp.float32),
        jnp.where(row == 1, middle.astype(jnp.float32), low.astype(jnp.float32)),
    ).astype(jnp.bfloat16)
    out_ref[:, 2 * PAIR :] = jnp.broadcast_to(spare, (out_ref.shape[0], SPARE, HD))


def finish(own, other, scaled_gain, gain_grad, places):
    group = 4
    spec = pl.BlockSpec((2, group, PAIR, HD), lambda i: (0, i, 0, 0))
    row = pl.BlockSpec((1, HD), lambda i: (0, 0))
    rows = 2 * PAIR + SPARE
    return pl.pallas_call(
        finish_kernel,
        grid=(places // group,),
        in_specs=[spec, spec, row, row],
        out_specs=pl.BlockSpec((group, rows, HD), lambda i: (i, 0, 0)),
        out_shape=jax.ShapeDtypeStruct((places, rows, HD), jnp.bfloat16),
        name="finish",
    )(own, other, scaled_gain, gain_grad)


def shards(queries, keys, values, key_gain, random_blocks, out_grad):
    heads = queries.shape[2] // HD
    places = lax.axis_size("seq")
    dp = lax.axis_size("dp")
    core = lax.axis_index("dp") % 2
    cores = core.reshape(1)
    head = lax.axis_index("seq") % heads

    def swap(x, bit=1):
        return lax.ppermute(x, "dp", [(i, i ^ bit) for i in range(dp)])

    def over_seq(x):
        return lax.all_to_all(x, "seq", split_axis=0, concat_axis=0, tiled=True)

    def gather(arrays, spare):
        keep, send = pack(cores, arrays, spare, heads)
        both = lax.dynamic_update_slice(keep, swap(send)[None], (1 - core, 0, 0, 0))
        return both.reshape(places, keep.shape[2], HD)

    def scatter(x, count):
        x = x.reshape(2, heads, x.shape[1], HD)
        came = swap(lax.dynamic_index_in_dim(x, 1 - core, axis=0, keepdims=False))
        return unpack(cores, x, came, count)

    named = random_blocks.reshape(heads, 2, 2, NR).transpose(2, 0, 1, 3).reshape(2, heads, 1, 2 * NR)
    named = jnp.pad(named.astype(jnp.bfloat16), ((0, 0), (0, 0), (0, 0), (0, HD - 2 * NR)))
    gain = lax.dynamic_slice_in_dim(key_gain, head * HD, HD).reshape(1, HD)

    own = over_seq(gather((keys[0], values[0], queries[0]), named))
    grads_in = gather((out_grad[0],), None)
    own, grads_in = lax.optimization_barrier((own, grads_in))
    grads = over_seq(grads_in)
    other = swap(own)
    table = own[:, 3 * PAIR, : 2 * NR].astype(jnp.int32).reshape(2 * places * NR)

    att, weights, dense, keys_scaled = forward(cores, table, gain, own, other, places)
    att_back = over_seq(att)
    dq, part_own, part_other, gain_term = backward(
        cores, table, own, other, keys_scaled, grads, att, weights, dense, places
    )
    att_back, dq = lax.optimization_barrier((att_back, dq))
    dq_back = over_seq(dq)
    part_came = swap(part_other)
    bit = 1
    while bit < dp:
        gain_term = gain_term + swap(gain_term, bit)
        bit *= 2
    dkv = finish(part_own, part_came, gain * SCALE, gain_term[:1], places)
    dq_back, dkv = lax.optimization_barrier((dq_back, dkv))
    dkv_back = over_seq(dkv)
    (attended,) = scatter(att_back, 1)
    (query_grad,) = scatter(dq_back, 1)
    dkv_back, attended, query_grad = lax.optimization_barrier((dkv_back, attended, query_grad))
    key_grad, value_grad = scatter(dkv_back, 2)
    gain_rows = dkv_back[:, 2 * PAIR : 2 * PAIR + 3].astype(jnp.float32)
    gain_grad = jnp.sum(gain_rows.reshape(2, heads, 3, HD), axis=(0, 2)).reshape(heads * HD)
    return (attended[None], query_grad[None], key_grad[None], value_grad[None], gain_grad)


def solution(mesh):
    rows = P("dp", "seq", None)
    return jax.shard_map(
        shards,
        mesh=mesh,
        in_specs=(rows, rows, rows, P(), P(None, "seq", None), rows),
        out_specs=(rows, rows, rows, rows, P()),
        check_vma=False,
    )
```

```python
import functools
import math

import jax
import jax.numpy as jnp
from jax import lax
from jax.experimental import pallas as pl
from jax.experimental.pallas import tpu as pltpu
from jax.sharding import PartitionSpec as P

HD = 128
BLOCK = 64
NR = 3
NK = 8
PAIR = 2 * BLOCK
CHUNK = 4
WIDTH = CHUNK * PAIR
SPARE = 16
NEGATIVE = -1e30
SCALE = HD**-0.5
EXP_SCALE = SCALE * math.log2(math.e)
VMEM_LIMIT = 56 * 1024 * 1024


def nt(a, b):
    return lax.dot_general(a, b, (((1,), (1,)), ((), ())), preferred_element_type=jnp.float32)


def nn(a, b):
    return lax.dot_general(a, b, (((1,), (0,)), ((), ())), preferred_element_type=jnp.float32)


def tn(a, b):
    return lax.dot_general(a, b, (((0,), (0,)), ((), ())), preferred_element_type=jnp.float32)


def pack_kernel(group, count, with_spare, parity_ref, *refs):
    out_ref = refs[-1]
    for h in range(group):
        for slot in range(count):
            for turn in range(2):
                row = slot * PAIR + turn * BLOCK
                out_ref[h, row : row + BLOCK] = refs[2 * slot + turn][:, h * HD : (h + 1) * HD]
        if with_spare:
            out_ref[h, count * PAIR :] = jnp.broadcast_to(
                refs[2 * count][parity_ref[0], h], (SPARE, HD)
            )


def pack(parity, arrays, spare, heads, own):
    group = min(heads, 4)
    count = len(arrays)
    rows = count * PAIR + (SPARE if spare is not None else 0)
    specs = []
    args = []
    for array in arrays:
        for turn in range(2):
            specs.append(
                pl.BlockSpec((BLOCK, group * HD), lambda i, p, turn=turn: (2 * turn + p[0], i))
            )
            args.append(array)
    if spare is not None:
        specs.append(pl.BlockSpec((2, group, 1, HD), lambda i, p: (0, i, 0, 0)))
        args.append(spare)
    if own:
        shape = (2, heads, rows, HD)
        out_spec = pl.BlockSpec((pl.Squeezed(), group, rows, HD), lambda i, p: (p[0], i, 0, 0))
    else:
        shape = (heads, rows, HD)
        out_spec = pl.BlockSpec((group, rows, HD), lambda i, p: (i, 0, 0))
    size = 2 * heads * rows * HD
    return pl.pallas_call(
        functools.partial(pack_kernel, group, count, spare is not None),
        grid_spec=pltpu.PrefetchScalarGridSpec(
            num_scalar_prefetch=1,
            grid=(heads // group,),
            in_specs=specs,
            out_specs=out_spec,
        ),
        out_shape=jax.ShapeDtypeStruct(shape, jnp.bfloat16),
        cost_estimate=pl.CostEstimate(flops=0, bytes_accessed=2 * size, transcendentals=0),
        name="pack_own" if own else "pack_sent",
    )(parity, *args)


def unpack_kernel(group, count, place_ref, *refs):
    out_refs = refs[-count:]
    for h in range(group):
        for slot in range(count):
            out_refs[slot][:, h * HD : (h + 1) * HD] = refs[slot][h]


def unpack(place, x, count, filled):
    heads = x.shape[-3]
    group = min(heads, 4)
    specs = []
    for slot in range(count):
        if filled is None:
            specs.append(
                pl.BlockSpec(
                    (pl.Squeezed(), group, BLOCK, HD),
                    lambda i, turn, p, slot=slot: (p[0], i, 2 * slot + turn, 0),
                )
            )
        else:
            specs.append(
                pl.BlockSpec(
                    (group, BLOCK, HD), lambda i, turn, p, slot=slot: (i, 2 * slot + turn, 0)
                )
            )
    args = [x] * count
    aliases = {}
    if filled is not None:
        aliases = {1 + count + slot: slot for slot in range(count)}
        specs += [pl.BlockSpec(memory_space=pl.ANY)] * count
        args += list(filled)
    out_spec = pl.BlockSpec((BLOCK, group * HD), lambda i, turn, p: (2 * turn + p[0], i))
    size = 2 * count * heads * PAIR * HD
    return pl.pallas_call(
        functools.partial(unpack_kernel, group, count),
        grid_spec=pltpu.PrefetchScalarGridSpec(
            num_scalar_prefetch=1,
            grid=(heads // group, 2),
            in_specs=specs,
            out_specs=[out_spec] * count,
        ),
        out_shape=[jax.ShapeDtypeStruct((4 * BLOCK, heads * HD), x.dtype)] * count,
        input_output_aliases=aliases,
        cost_estimate=pl.CostEstimate(flops=0, bytes_accessed=2 * size, transcendentals=0),
        name="unpack_own" if filled is None else "unpack_sent",
    )(place, *args)


def locate(block):
    half = block // 2
    return (block % 2, half // 2, pl.ds(pl.multiple_of((half % 2) * BLOCK, BLOCK), BLOCK))


def key_places(table_ref, n, block, total_blocks):
    return [
        (0, 0, pl.ds(0, BLOCK)),
        (1, 0, pl.ds(0, BLOCK)),
        locate(jnp.maximum(block - 1, 0)),
        locate(block),
        locate(jnp.minimum(block + 1, total_blocks - 1)),
    ] + [locate(table_ref[n * NR + r]) for r in range(NR)]


def chunk_rows(ref, t, steps):
    return ref[t // steps, pl.ds((t % steps) * CHUNK, CHUNK)].reshape(WIDTH, HD)


def forward_kernel(
    places,
    unroll,
    core_ref,
    table_ref,
    gain_ref,
    own_ref,
    other_ref,
    att_ref,
    weight_ref,
    dense_ref,
    key_out,
    k_scr,
    v_scr,
    q_scr,
    score_scr,
    weight_scr,
    dense_scr,
    in_sem,
    out_sem,
    weight_sem,
):
    core = core_ref[0]
    total_blocks = 4 * places
    steps = places // CHUNK

    def rows(ref, slot):
        return ref.at[:, slot * PAIR : (slot + 1) * PAIR]

    copies = [
        pltpu.make_async_copy(rows(own_ref, 0), k_scr.at[core], in_sem.at[0]),
        pltpu.make_async_copy(rows(other_ref, 0), k_scr.at[1 - core], in_sem.at[1]),
        pltpu.make_async_copy(rows(own_ref, 2), q_scr, in_sem.at[2]),
        pltpu.make_async_copy(rows(own_ref, 1), v_scr.at[core], in_sem.at[3]),
        pltpu.make_async_copy(rows(other_ref, 1), v_scr.at[1 - core], in_sem.at[4]),
    ]
    for copy in copies:
        copy.start()
    for copy in copies[:3]:
        copy.wait()

    gain = gain_ref[...]
    query = q_scr[0, :BLOCK]

    def lanes(x, op):
        out = x[:, :HD]
        for t in range(1, WIDTH // HD):
            out = op(out, x[:, t * HD : (t + 1) * HD])
        return out

    def dense_scores(t, top):
        where = (t // steps, pl.ds((t % steps) * CHUNK, CHUNK))
        keys = (k_scr[where].astype(jnp.float32) * gain).astype(jnp.bfloat16)
        k_scr[where] = keys
        scores = nt(query, keys.reshape(WIDTH, HD))
        score_scr[t] = scores
        return jnp.maximum(top, lanes(scores, jnp.maximum))

    top = lax.fori_loop(
        0, 2 * steps, dense_scores, jnp.full((BLOCK, HD), NEGATIVE, jnp.float32), unroll=4
    )
    top = jnp.max(top, axis=1, keepdims=True)
    key_copy = pltpu.make_async_copy(k_scr, key_out, out_sem.at[0])
    key_copy.start()
    for copy in copies[3:]:
        copy.wait()

    def dense_expo(t, carry):
        total, numer = carry
        expo = jnp.exp2((score_scr[t] - top) * EXP_SCALE)
        score_scr[t] = expo
        numer = numer + nn(expo.astype(jnp.bfloat16), chunk_rows(v_scr, t, steps))
        return total + lanes(expo, jnp.add), numer

    zero = jnp.zeros((BLOCK, HD), jnp.float32)
    total, numer = lax.fori_loop(0, 2 * steps, dense_expo, (zero, zero), unroll=4)
    inverse = 1.0 / jnp.sum(total, axis=1, keepdims=True)
    att_ref[0, :BLOCK] = (numer * inverse).astype(jnp.bfloat16)

    def dense_weights(t, carry):
        dense_scr[t] = (score_scr[t] * inverse).astype(jnp.bfloat16)
        return carry

    lax.fori_loop(0, 2 * steps, dense_weights, 0, unroll=4)

    dense_copy = pltpu.make_async_copy(dense_scr, dense_ref, out_sem.at[1])
    dense_copy.start()
    column = lax.broadcasted_iota(jnp.int32, (1, NK * BLOCK), 1) // BLOCK

    def sparse_block(n):
        block = 2 * n + core
        listing = key_places(table_ref, n, block, total_blocks)
        key_list = jnp.concatenate([k_scr[where] for where in listing], axis=0)
        value_list = jnp.concatenate([v_scr[where] for where in listing], axis=0)
        mine = (n // 2, pl.ds(pl.multiple_of((n % 2) * BLOCK, BLOCK), BLOCK))
        masked = ((column == 2) & (block == 2)) | ((column == 4) & (block == total_blocks - 1))
        scores = nt(q_scr[mine], key_list) + jnp.where(masked, NEGATIVE, 0.0)
        top = jnp.max(scores, axis=1, keepdims=True)
        expo = jnp.exp2((scores - top) * EXP_SCALE)
        inverse = 1.0 / jnp.sum(expo, axis=1, keepdims=True)
        numer = nn(expo.astype(jnp.bfloat16), value_list)
        return mine, (numer * inverse).astype(jnp.bfloat16), (expo * inverse).astype(jnp.bfloat16)

    def sparse_step(t, carry):
        first = 1 + t * unroll
        done = [sparse_block(first + u) for u in range(unroll)]
        for u, (mine, attended, weights) in enumerate(done):
            att_ref[mine] = attended
            weight_scr[first + u] = weights
        weight_copy(t).start()
        return carry

    def weight_copy(t):
        part = pl.ds(1 + t * unroll, unroll)
        return pltpu.make_async_copy(weight_scr.at[part], weight_ref.at[part], weight_sem.at[t])

    rounds = (2 * places - 1) // unroll
    lax.fori_loop(0, rounds, sparse_step, 0)
    key_copy.wait()
    dense_copy.wait()
    for t in range(rounds):
        weight_copy(t).wait()


def forward(core, table, gain, own, other, places):
    unroll = 9 if (2 * places - 1) % 9 == 0 else 1
    both = (2, places, PAIR, HD)
    smem = pl.BlockSpec(memory_space=pltpu.SMEM)
    vmem = pl.BlockSpec(memory_space=pltpu.VMEM)
    hbm = pl.BlockSpec(memory_space=pl.ANY)
    blocks = 2 * places
    return pl.pallas_call(
        functools.partial(forward_kernel, places, unroll),
        in_specs=[smem, smem, vmem, hbm, hbm],
        out_specs=[vmem, hbm, hbm, hbm],
        out_shape=[
            jax.ShapeDtypeStruct((places, PAIR, HD), jnp.bfloat16),
            jax.ShapeDtypeStruct((blocks, BLOCK, NK * BLOCK), jnp.bfloat16),
            jax.ShapeDtypeStruct((places // 2, BLOCK, WIDTH), jnp.bfloat16),
            jax.ShapeDtypeStruct(both, jnp.bfloat16),
        ],
        scratch_shapes=[
            pltpu.VMEM(both, jnp.bfloat16),
            pltpu.VMEM(both, jnp.bfloat16),
            pltpu.VMEM((places, PAIR, HD), jnp.bfloat16),
            pltpu.VMEM((places // 2, BLOCK, WIDTH), jnp.float32),
            pltpu.VMEM((blocks, BLOCK, NK * BLOCK), jnp.bfloat16),
            pltpu.VMEM((places // 2, BLOCK, WIDTH), jnp.bfloat16),
            pltpu.SemaphoreType.DMA((5,)),
            pltpu.SemaphoreType.DMA((2,)),
            pltpu.SemaphoreType.DMA(((blocks - 1) // unroll,)),
        ],
        compiler_params=pltpu.CompilerParams(vmem_limit_bytes=VMEM_LIMIT),
        cost_estimate=pl.CostEstimate(
            flops=4 * blocks * BLOCK * HD * 3 * NK * BLOCK,
            bytes_accessed=60 << 20,
            transcendentals=blocks * BLOCK * NK * BLOCK,
        ),
        name="forward",
    )(core, table, gain, own, other)


def diagonal(query, grad):
    zero = jnp.zeros_like(query)
    return jnp.concatenate(
        [jnp.concatenate([query, zero], axis=1), jnp.concatenate([zero, grad], axis=1)], axis=0
    )


def joint_terms(dscores, weights, operand):
    return tn(jnp.concatenate([dscores, weights], axis=0), operand)


def backward_kernel(
    places,
    unroll,
    core_ref,
    table_ref,
    own_ref,
    other_ref,
    key_ref,
    grad_ref,
    att_ref,
    weight_ref,
    dense_ref,
    dq_ref,
    own_out,
    other_out,
    gain_out,
    k_scr,
    v_scr,
    q_scr,
    g_scr,
    a_scr,
    weight_scr,
    dense_scr,
    acc_k,
    acc_v,
    raw_scr,
    in_sem,
    out_sem,
):
    core = core_ref[0]
    total_blocks = 4 * places
    steps = places // CHUNK

    def rows(ref, slot):
        return ref.at[:, slot * PAIR : (slot + 1) * PAIR]

    copies = [
        pltpu.make_async_copy(src, dst, in_sem.at[at])
        for at, (src, dst) in enumerate(
            [
                (grad_ref, g_scr),
                (att_ref, a_scr),
                (dense_ref, dense_scr),
                (rows(own_ref, 1), v_scr.at[core]),
                (rows(other_ref, 1), v_scr.at[1 - core]),
                (key_ref, k_scr),
                (rows(own_ref, 2), q_scr),
                (weight_ref, weight_scr),
                (rows(own_ref, 0), raw_scr.at[core]),
                (rows(other_ref, 0), raw_scr.at[1 - core]),
            ]
        )
    ]
    for copy in copies:
        copy.start()
    for copy in copies[:7]:
        copy.wait()

    def row_delta(grad, attended):
        return jnp.sum(
            grad.astype(jnp.float32) * attended.astype(jnp.float32), axis=1, keepdims=True
        )

    query = q_scr[0, :BLOCK]
    grad = g_scr[0, :BLOCK]
    delta = row_delta(grad, a_scr[0, :BLOCK])
    operand = diagonal(query, grad)

    def dense_back(t, dquery):
        weights = dense_scr[t]
        dprobs = nt(grad, chunk_rows(v_scr, t, steps))
        dscores = (weights.astype(jnp.float32) * (dprobs - delta)).astype(jnp.bfloat16)
        where = (t // steps, pl.ds((t % steps) * CHUNK, CHUNK))
        both = joint_terms(dscores, weights, operand)
        acc_k[where] = both[:, :HD].reshape(CHUNK, PAIR, HD)
        acc_v[where] = both[:, HD:].reshape(CHUNK, PAIR, HD)
        return dquery + nn(dscores, chunk_rows(k_scr, t, steps))

    zero = jnp.zeros((BLOCK, HD), jnp.float32)
    dquery = lax.fori_loop(0, 2 * steps, dense_back, zero, unroll=4)
    dq_ref[0, :BLOCK] = (dquery * SCALE).astype(jnp.bfloat16)
    copies[7].wait()

    def sparse_block(n):
        block = 2 * n + core
        listing = key_places(table_ref, n, block, total_blocks)
        key_list = jnp.concatenate([k_scr[where] for where in listing], axis=0)
        value_list = jnp.concatenate([v_scr[where] for where in listing], axis=0)
        mine = (n // 2, pl.ds(pl.multiple_of((n % 2) * BLOCK, BLOCK), BLOCK))
        grad = g_scr[mine]
        weights = weight_scr[n]
        delta = row_delta(grad, a_scr[mine])
        dprobs = nt(grad, value_list)
        dscores = (weights.astype(jnp.float32) * (dprobs - delta)).astype(jnp.bfloat16)
        dquery = nn(dscores, key_list)
        return listing, mine, dquery, joint_terms(dscores, weights, diagonal(q_scr[mine], grad))

    def sparse_step(t, carry):
        done = [sparse_block(1 + t * unroll + u) for u in range(unroll)]
        for listing, mine, dquery, terms in done:
            dq_ref[mine] = (dquery * SCALE).astype(jnp.bfloat16)
            for slot, where in enumerate(listing):
                acc_k[where] += terms[slot * BLOCK : (slot + 1) * BLOCK, :HD]
                acc_v[where] += terms[slot * BLOCK : (slot + 1) * BLOCK, HD:]
        return carry

    lax.fori_loop(0, (2 * places - 1) // unroll, sparse_step, 0)
    for copy in copies[8:]:
        copy.wait()

    copies = [
        pltpu.make_async_copy(acc_k.at[core], own_out.at[0], out_sem.at[0]),
        pltpu.make_async_copy(acc_v.at[core], own_out.at[1], out_sem.at[1]),
    ]
    for copy in copies:
        copy.start()

    def round_other(t, carry):
        where = pl.ds(t * CHUNK, CHUNK)
        mine = acc_k[core, where] * raw_scr[core, where].astype(jnp.float32)
        far = acc_k[1 - core, where]
        theirs = far * raw_scr[1 - core, where].astype(jnp.float32)
        other_out[0, where] = far.astype(jnp.bfloat16)
        other_out[1, where] = acc_v[1 - core, where].astype(jnp.bfloat16)
        return carry + jnp.sum((mine + theirs).reshape(CHUNK * PAIR // 8, 8, HD), axis=0)

    gain_term = lax.fori_loop(0, steps, round_other, jnp.zeros((8, HD), jnp.float32), unroll=2)
    gain_term = jnp.sum(gain_term, axis=0, keepdims=True) * SCALE
    gain_out[...] = jnp.broadcast_to(gain_term, (8, HD))
    for copy in copies:
        copy.wait()


def backward(core, table, own, other, keys, grads, att, weights, dense, places):
    unroll = 9 if (2 * places - 1) % 9 == 0 else 1
    both = (2, places, PAIR, HD)
    half = (places, PAIR, HD)
    blocks = 2 * places
    smem = pl.BlockSpec(memory_space=pltpu.SMEM)
    vmem = pl.BlockSpec(memory_space=pltpu.VMEM)
    hbm = pl.BlockSpec(memory_space=pl.ANY)
    return pl.pallas_call(
        functools.partial(backward_kernel, places, unroll),
        in_specs=[smem, smem] + [hbm] * 7,
        out_specs=[vmem, hbm, vmem, vmem],
        out_shape=[
            jax.ShapeDtypeStruct(half, jnp.bfloat16),
            jax.ShapeDtypeStruct(both, jnp.float32),
            jax.ShapeDtypeStruct(both, jnp.bfloat16),
            jax.ShapeDtypeStruct((8, HD), jnp.float32),
        ],
        scratch_shapes=[
            pltpu.VMEM(both, jnp.bfloat16),
            pltpu.VMEM(both, jnp.bfloat16),
            pltpu.VMEM(half, jnp.bfloat16),
            pltpu.VMEM(half, jnp.bfloat16),
            pltpu.VMEM(half, jnp.bfloat16),
            pltpu.VMEM(weights.shape, jnp.bfloat16),
            pltpu.VMEM(dense.shape, jnp.bfloat16),
            pltpu.VMEM(both, jnp.float32),
            pltpu.VMEM(both, jnp.float32),
            pltpu.VMEM(both, jnp.bfloat16),
            pltpu.SemaphoreType.DMA((10,)),
            pltpu.SemaphoreType.DMA((2,)),
        ],
        compiler_params=pltpu.CompilerParams(vmem_limit_bytes=VMEM_LIMIT),
        cost_estimate=pl.CostEstimate(
            flops=8 * blocks * BLOCK * HD * 3 * NK * BLOCK,
            bytes_accessed=100 << 20,
            transcendentals=0,
        ),
        name="backward",
    )(core, table, own, other, keys, grads, att, weights, dense)


def finish_kernel(own_ref, other_ref, scaled_gain_ref, gain_grad_ref, out_ref):
    gain = scaled_gain_ref[...]
    dkey = own_ref[0] + other_ref[0].astype(jnp.float32)
    out_ref[:, :PAIR] = (dkey * gain).astype(jnp.bfloat16)
    dvalue = own_ref[1] + other_ref[1].astype(jnp.float32)
    out_ref[:, PAIR : 2 * PAIR] = dvalue.astype(jnp.bfloat16)
    total = gain_grad_ref[...]
    high = total.astype(jnp.bfloat16)
    rest = total - high.astype(jnp.float32)
    middle = rest.astype(jnp.bfloat16)
    low = (rest - middle.astype(jnp.float32)).astype(jnp.bfloat16)
    row = lax.broadcasted_iota(jnp.int32, (SPARE, HD), 0)
    spare = jnp.where(
        row == 0,
        high.astype(jnp.float32),
        jnp.where(row == 1, middle.astype(jnp.float32), low.astype(jnp.float32)),
    ).astype(jnp.bfloat16)
    out_ref[:, 2 * PAIR :] = jnp.broadcast_to(spare, (out_ref.shape[0], SPARE, HD))


def finish(own, other, scaled_gain, gain_grad, places):
    group = 4
    spec = pl.BlockSpec((2, group, PAIR, HD), lambda i: (0, i, 0, 0))
    row = pl.BlockSpec((1, HD), lambda i: (0, 0))
    rows = 2 * PAIR + SPARE
    return pl.pallas_call(
        finish_kernel,
        grid=(places // group,),
        in_specs=[spec, spec, row, row],
        out_specs=pl.BlockSpec((group, rows, HD), lambda i: (i, 0, 0)),
        out_shape=jax.ShapeDtypeStruct((places, rows, HD), jnp.bfloat16),
        name="finish",
    )(own, other, scaled_gain, gain_grad)


def shards(queries, keys, values, key_gain, random_blocks, out_grad):
    heads = queries.shape[2] // HD
    places = lax.axis_size("seq")
    dp = lax.axis_size("dp")
    core = lax.axis_index("dp") % 2
    cores = core.reshape(1)
    head = lax.axis_index("seq") % heads

    def swap(x, bit=1):
        return lax.ppermute(x, "dp", [(i, i ^ bit) for i in range(dp)])

    def over_seq(x):
        return lax.all_to_all(x, "seq", split_axis=0, concat_axis=0, tiled=True)

    def gather(arrays, spare):
        came = swap(pack(1 - cores, arrays, spare, heads, False))
        both = pack(cores, arrays, spare, heads, True)
        both = lax.dynamic_update_slice(both, came[None], (1 - core, 0, 0, 0))
        return both.reshape(places, both.shape[2], HD)

    def scatter(x, count):
        x = x.reshape(2, heads, x.shape[1], HD)
        came = swap(lax.dynamic_index_in_dim(x, 1 - core, axis=0, keepdims=False))
        return unpack(1 - cores, came, count, unpack(cores, x, count, None))

    named = random_blocks.reshape(heads, 2, 2, NR).transpose(2, 0, 1, 3).reshape(2, heads, 1, 2 * NR)
    named = jnp.pad(named.astype(jnp.bfloat16), ((0, 0), (0, 0), (0, 0), (0, HD - 2 * NR)))
    gain = lax.dynamic_slice_in_dim(key_gain, head * HD, HD).reshape(1, HD)

    own = over_seq(gather((keys[0], values[0], queries[0]), named))
    grads_in = gather((out_grad[0],), None)
    own, grads_in = lax.optimization_barrier((own, grads_in))
    grads = over_seq(grads_in)
    other = swap(own)
    table = own[:, 3 * PAIR, : 2 * NR].astype(jnp.int32).reshape(2 * places * NR)

    att, weights, dense, keys_scaled = forward(cores, table, gain, own, other, places)
    att_back = over_seq(att)
    dq, part_own, part_other, gain_term = backward(
        cores, table, own, other, keys_scaled, grads, att, weights, dense, places
    )
    att_back, dq = lax.optimization_barrier((att_back, dq))
    dq_back = over_seq(dq)
    part_came = swap(part_other)
    bit = 1
    while bit < dp:
        gain_term = gain_term + swap(gain_term, bit)
        bit *= 2
    dkv = finish(part_own, part_came, gain * SCALE, gain_term[:1], places)
    dq_back, dkv = lax.optimization_barrier((dq_back, dkv))
    dkv_back = over_seq(dkv)
    (attended,) = scatter(att_back, 1)
    (query_grad,) = scatter(dq_back, 1)
    dkv_back, attended, query_grad = lax.optimization_barrier((dkv_back, attended, query_grad))
    key_grad, value_grad = scatter(dkv_back, 2)
    gain_rows = dkv_back[:, 2 * PAIR : 2 * PAIR + 3].astype(jnp.float32)
    gain_grad = jnp.sum(gain_rows.reshape(2, heads, 3, HD), axis=(0, 2)).reshape(heads * HD)
    return (attended[None], query_grad[None], key_grad[None], value_grad[None], gain_grad)


def solution(mesh):
    rows = P("dp", "seq", None)
    return jax.shard_map(
        shards,
        mesh=mesh,
        in_specs=(rows, rows, rows, P(), P(None, "seq", None), rows),
        out_specs=(rows, rows, rows, rows, P()),
        check_vma=False,
    )
```

```python
import functools
import math

import jax
import jax.numpy as jnp
from jax import lax
from jax.experimental import pallas as pl
from jax.experimental.pallas import tpu as pltpu
from jax.sharding import PartitionSpec as P

HD = 128
BLOCK = 64
NR = 3
NK = 8
PAIR = 2 * BLOCK
CHUNK = 4
WIDTH = CHUNK * PAIR
SPARE = 8
NEGATIVE = -1e30
SCALE = HD**-0.5
EXP_SCALE = SCALE * math.log2(math.e)
VMEM_LIMIT = 56 * 1024 * 1024


def nt(a, b):
    return lax.dot_general(a, b, (((1,), (1,)), ((), ())), preferred_element_type=jnp.float32)


def nn(a, b):
    return lax.dot_general(a, b, (((1,), (0,)), ((), ())), preferred_element_type=jnp.float32)


def tn(a, b):
    return lax.dot_general(a, b, (((0,), (0,)), ((), ())), preferred_element_type=jnp.float32)


def pack_kernel(group, count, with_spare, parity_ref, *refs):
    out_ref = refs[-1]
    for h in range(group):
        for slot in range(count):
            for turn in range(2):
                row = slot * PAIR + turn * BLOCK
                out_ref[h, row : row + BLOCK] = refs[2 * slot + turn][:, h * HD : (h + 1) * HD]
        if with_spare:
            out_ref[h, count * PAIR :] = jnp.broadcast_to(
                refs[2 * count][parity_ref[0], h], (SPARE, HD)
            )


def pack(parity, arrays, spare, heads, own):
    group = min(heads, 8)
    count = len(arrays)
    rows = count * PAIR + (SPARE if spare is not None else 0)
    specs = []
    args = []
    for array in arrays:
        for turn in range(2):
            specs.append(
                pl.BlockSpec((BLOCK, group * HD), lambda i, p, turn=turn: (2 * turn + p[0], i))
            )
            args.append(array)
    if spare is not None:
        specs.append(pl.BlockSpec((2, group, 1, HD), lambda i, p: (0, i, 0, 0)))
        args.append(spare)
    if own:
        shape = (2, heads, rows, HD)
        out_spec = pl.BlockSpec((pl.Squeezed(), group, rows, HD), lambda i, p: (p[0], i, 0, 0))
    else:
        shape = (heads, rows, HD)
        out_spec = pl.BlockSpec((group, rows, HD), lambda i, p: (i, 0, 0))
    size = 2 * heads * rows * HD
    return pl.pallas_call(
        functools.partial(pack_kernel, group, count, spare is not None),
        grid_spec=pltpu.PrefetchScalarGridSpec(
            num_scalar_prefetch=1,
            grid=(heads // group,),
            in_specs=specs,
            out_specs=out_spec,
        ),
        out_shape=jax.ShapeDtypeStruct(shape, jnp.bfloat16),
        cost_estimate=pl.CostEstimate(flops=0, bytes_accessed=2 * size, transcendentals=0),
        name="pack_own" if own else "pack_sent",
    )(parity, *args)


def unpack_kernel(group, core_ref, keep_ref, came_ref, *out_refs):
    core = core_ref[0]
    for in_ref, parity in ((keep_ref, core), (came_ref, 1 - core)):
        for h in range(group):
            for slot, ref in enumerate(out_refs):
                for turn in range(2):
                    row = slot * PAIR + turn * BLOCK
                    at = pl.multiple_of((2 * turn + parity) * BLOCK, BLOCK)
                    ref[pl.ds(at, BLOCK), h * HD : (h + 1) * HD] = in_ref[h, row : row + BLOCK]


def unpack(core, keep, came, count):
    heads, rows = keep.shape[1:3]
    group = min(heads, 8)
    return pl.pallas_call(
        functools.partial(unpack_kernel, group),
        grid_spec=pltpu.PrefetchScalarGridSpec(
            num_scalar_prefetch=1,
            grid=(heads // group,),
            in_specs=[
                pl.BlockSpec((pl.Squeezed(), group, rows, HD), lambda i, c: (c[0], i, 0, 0)),
                pl.BlockSpec((group, rows, HD), lambda i, c: (i, 0, 0)),
            ],
            out_specs=[pl.BlockSpec((4 * BLOCK, group * HD), lambda i, c: (0, i))] * count,
        ),
        out_shape=[jax.ShapeDtypeStruct((4 * BLOCK, heads * HD), keep.dtype)] * count,
        cost_estimate=pl.CostEstimate(
            flops=0, bytes_accessed=16 * count * BLOCK * heads * HD, transcendentals=0
        ),
        name="unpack",
    )(core, keep, came)


def locate(block):
    half = block // 2
    return (block % 2, half // 2, pl.ds(pl.multiple_of((half % 2) * BLOCK, BLOCK), BLOCK))


def key_places(table_ref, n, block, total_blocks):
    return [
        (0, 0, pl.ds(0, BLOCK)),
        (1, 0, pl.ds(0, BLOCK)),
        locate(jnp.maximum(block - 1, 0)),
        locate(block),
        locate(jnp.minimum(block + 1, total_blocks - 1)),
    ] + [locate(table_ref[n * NR + r]) for r in range(NR)]


def chunk_rows(ref, t, steps):
    return ref[t // steps, pl.ds((t % steps) * CHUNK, CHUNK)].reshape(WIDTH, HD)


def forward_kernel(
    places,
    unroll,
    core_ref,
    table_ref,
    gain_ref,
    own_ref,
    other_ref,
    att_ref,
    weight_ref,
    dense_ref,
    key_out,
    k_scr,
    v_scr,
    q_scr,
    score_scr,
    weight_scr,
    dense_scr,
    in_sem,
    out_sem,
    weight_sem,
):
    core = core_ref[0]
    total_blocks = 4 * places
    steps = places // CHUNK

    def rows(ref, slot):
        return ref.at[:, slot * PAIR : (slot + 1) * PAIR]

    copies = [
        pltpu.make_async_copy(rows(own_ref, 0), k_scr.at[core], in_sem.at[0]),
        pltpu.make_async_copy(rows(other_ref, 0), k_scr.at[1 - core], in_sem.at[1]),
        pltpu.make_async_copy(rows(own_ref, 2), q_scr, in_sem.at[2]),
        pltpu.make_async_copy(rows(own_ref, 1), v_scr.at[core], in_sem.at[3]),
        pltpu.make_async_copy(rows(other_ref, 1), v_scr.at[1 - core], in_sem.at[4]),
    ]
    for copy in copies:
        copy.start()
    for copy in copies[:3]:
        copy.wait()

    gain = gain_ref[...]
    query = q_scr[0, :BLOCK]

    def lanes(x, op):
        out = x[:, :HD]
        for t in range(1, WIDTH // HD):
            out = op(out, x[:, t * HD : (t + 1) * HD])
        return out

    def dense_scores(t, top):
        where = (t // steps, pl.ds((t % steps) * CHUNK, CHUNK))
        keys = (k_scr[where].astype(jnp.float32) * gain).astype(jnp.bfloat16)
        k_scr[where] = keys
        scores = nt(query, keys.reshape(WIDTH, HD))
        score_scr[t] = scores
        return jnp.maximum(top, lanes(scores, jnp.maximum))

    top = lax.fori_loop(
        0, 2 * steps, dense_scores, jnp.full((BLOCK, HD), NEGATIVE, jnp.float32), unroll=4
    )
    top = jnp.max(top, axis=1, keepdims=True)
    key_copy = pltpu.make_async_copy(k_scr, key_out, out_sem.at[0])
    key_copy.start()
    for copy in copies[3:]:
        copy.wait()

    def dense_expo(t, carry):
        total, numer = carry
        expo = jnp.exp2((score_scr[t] - top) * EXP_SCALE)
        score_scr[t] = expo
        numer = numer + nn(expo.astype(jnp.bfloat16), chunk_rows(v_scr, t, steps))
        return total + lanes(expo, jnp.add), numer

    zero = jnp.zeros((BLOCK, HD), jnp.float32)
    total, numer = lax.fori_loop(0, 2 * steps, dense_expo, (zero, zero), unroll=4)
    inverse = 1.0 / jnp.sum(total, axis=1, keepdims=True)
    att_ref[0, :BLOCK] = (numer * inverse).astype(jnp.bfloat16)

    def dense_weights(t, carry):
        dense_scr[t] = (score_scr[t] * inverse).astype(jnp.bfloat16)
        return carry

    lax.fori_loop(0, 2 * steps, dense_weights, 0, unroll=4)

    dense_copy = pltpu.make_async_copy(dense_scr, dense_ref, out_sem.at[1])
    dense_copy.start()
    column = lax.broadcasted_iota(jnp.int32, (1, NK * BLOCK), 1) // BLOCK

    def sparse_block(n):
        block = 2 * n + core
        listing = key_places(table_ref, n, block, total_blocks)
        key_list = jnp.concatenate([k_scr[where] for where in listing], axis=0)
        value_list = jnp.concatenate([v_scr[where] for where in listing], axis=0)
        mine = (n // 2, pl.ds(pl.multiple_of((n % 2) * BLOCK, BLOCK), BLOCK))
        masked = ((column == 2) & (block == 2)) | ((column == 4) & (block == total_blocks - 1))
        scores = nt(q_scr[mine], key_list) + jnp.where(masked, NEGATIVE, 0.0)
        top = jnp.max(scores, axis=1, keepdims=True)
        expo = jnp.exp2((scores - top) * EXP_SCALE)
        inverse = 1.0 / jnp.sum(expo, axis=1, keepdims=True)
        numer = nn(expo.astype(jnp.bfloat16), value_list)
        return mine, (numer * inverse).astype(jnp.bfloat16), (expo * inverse).astype(jnp.bfloat16)

    def sparse_step(t, carry):
        first = 1 + t * unroll
        done = [sparse_block(first + u) for u in range(unroll)]
        for u, (mine, attended, weights) in enumerate(done):
            att_ref[mine] = attended
            weight_scr[first + u] = weights
        weight_copy(t).start()
        return carry

    def weight_copy(t):
        part = pl.ds(1 + t * unroll, unroll)
        return pltpu.make_async_copy(weight_scr.at[part], weight_ref.at[part], weight_sem.at[t])

    rounds = (2 * places - 1) // unroll
    lax.fori_loop(0, rounds, sparse_step, 0)
    key_copy.wait()
    dense_copy.wait()
    for t in range(rounds):
        weight_copy(t).wait()


def forward(core, table, gain, own, other, places):
    unroll = 9 if (2 * places - 1) % 9 == 0 else 1
    both = (2, places, PAIR, HD)
    smem = pl.BlockSpec(memory_space=pltpu.SMEM)
    vmem = pl.BlockSpec(memory_space=pltpu.VMEM)
    hbm = pl.BlockSpec(memory_space=pl.ANY)
    blocks = 2 * places
    return pl.pallas_call(
        functools.partial(forward_kernel, places, unroll),
        in_specs=[smem, smem, vmem, hbm, hbm],
        out_specs=[vmem, hbm, hbm, hbm],
        out_shape=[
            jax.ShapeDtypeStruct((places, PAIR, HD), jnp.bfloat16),
            jax.ShapeDtypeStruct((blocks, BLOCK, NK * BLOCK), jnp.bfloat16),
            jax.ShapeDtypeStruct((places // 2, BLOCK, WIDTH), jnp.bfloat16),
            jax.ShapeDtypeStruct(both, jnp.bfloat16),
        ],
        scratch_shapes=[
            pltpu.VMEM(both, jnp.bfloat16),
            pltpu.VMEM(both, jnp.bfloat16),
            pltpu.VMEM((places, PAIR, HD), jnp.bfloat16),
            pltpu.VMEM((places // 2, BLOCK, WIDTH), jnp.float32),
            pltpu.VMEM((blocks, BLOCK, NK * BLOCK), jnp.bfloat16),
            pltpu.VMEM((places // 2, BLOCK, WIDTH), jnp.bfloat16),
            pltpu.SemaphoreType.DMA((5,)),
            pltpu.SemaphoreType.DMA((2,)),
            pltpu.SemaphoreType.DMA(((blocks - 1) // unroll,)),
        ],
        compiler_params=pltpu.CompilerParams(vmem_limit_bytes=VMEM_LIMIT),
        cost_estimate=pl.CostEstimate(
            flops=4 * blocks * BLOCK * HD * 3 * NK * BLOCK,
            bytes_accessed=60 << 20,
            transcendentals=blocks * BLOCK * NK * BLOCK,
        ),
        name="forward",
    )(core, table, gain, own, other)


def diagonal(query, grad):
    zero = jnp.zeros_like(query)
    return jnp.concatenate(
        [jnp.concatenate([query, zero], axis=1), jnp.concatenate([zero, grad], axis=1)], axis=0
    )


def joint_terms(dscores, weights, operand):
    return tn(jnp.concatenate([dscores, weights], axis=0), operand)


def backward_kernel(
    places,
    unroll,
    core_ref,
    table_ref,
    own_ref,
    other_ref,
    key_ref,
    grad_ref,
    att_ref,
    weight_ref,
    dense_ref,
    dq_ref,
    own_out,
    other_out,
    gain_out,
    k_scr,
    v_scr,
    q_scr,
    g_scr,
    a_scr,
    weight_scr,
    dense_scr,
    acc_k,
    acc_v,
    raw_scr,
    in_sem,
    out_sem,
):
    core = core_ref[0]
    total_blocks = 4 * places
    steps = places // CHUNK

    def rows(ref, slot):
        return ref.at[:, slot * PAIR : (slot + 1) * PAIR]

    copies = [
        pltpu.make_async_copy(src, dst, in_sem.at[at])
        for at, (src, dst) in enumerate(
            [
                (grad_ref, g_scr),
                (att_ref, a_scr),
                (dense_ref, dense_scr),
                (rows(own_ref, 1), v_scr.at[core]),
                (rows(other_ref, 1), v_scr.at[1 - core]),
                (key_ref, k_scr),
                (rows(own_ref, 2), q_scr),
                (weight_ref, weight_scr),
                (rows(own_ref, 0), raw_scr.at[core]),
                (rows(other_ref, 0), raw_scr.at[1 - core]),
            ]
        )
    ]
    for copy in copies:
        copy.start()
    for copy in copies[:7]:
        copy.wait()

    def row_delta(grad, attended):
        return jnp.sum(
            grad.astype(jnp.float32) * attended.astype(jnp.float32), axis=1, keepdims=True
        )

    query = q_scr[0, :BLOCK]
    grad = g_scr[0, :BLOCK]
    delta = row_delta(grad, a_scr[0, :BLOCK])
    operand = diagonal(query, grad)

    def dense_back(t, dquery):
        weights = dense_scr[t]
        dprobs = nt(grad, chunk_rows(v_scr, t, steps))
        dscores = (weights.astype(jnp.float32) * (dprobs - delta)).astype(jnp.bfloat16)
        where = (t // steps, pl.ds((t % steps) * CHUNK, CHUNK))
        both = joint_terms(dscores, weights, operand)
        acc_k[where] = both[:, :HD].reshape(CHUNK, PAIR, HD)
        acc_v[where] = both[:, HD:].reshape(CHUNK, PAIR, HD)
        return dquery + nn(dscores, chunk_rows(k_scr, t, steps))

    zero = jnp.zeros((BLOCK, HD), jnp.float32)
    dquery = lax.fori_loop(0, 2 * steps, dense_back, zero, unroll=4)
    dq_ref[0, :BLOCK] = (dquery * SCALE).astype(jnp.bfloat16)
    copies[7].wait()

    def sparse_block(n):
        block = 2 * n + core
        listing = key_places(table_ref, n, block, total_blocks)
        key_list = jnp.concatenate([k_scr[where] for where in listing], axis=0)
        value_list = jnp.concatenate([v_scr[where] for where in listing], axis=0)
        mine = (n // 2, pl.ds(pl.multiple_of((n % 2) * BLOCK, BLOCK), BLOCK))
        grad = g_scr[mine]
        weights = weight_scr[n]
        delta = row_delta(grad, a_scr[mine])
        dprobs = nt(grad, value_list)
        dscores = (weights.astype(jnp.float32) * (dprobs - delta)).astype(jnp.bfloat16)
        dquery = nn(dscores, key_list)
        return listing, mine, dquery, joint_terms(dscores, weights, diagonal(q_scr[mine], grad))

    def sparse_step(t, carry):
        done = [sparse_block(1 + t * unroll + u) for u in range(unroll)]
        for listing, mine, dquery, terms in done:
            dq_ref[mine] = (dquery * SCALE).astype(jnp.bfloat16)
            for slot, where in enumerate(listing):
                acc_k[where] += terms[slot * BLOCK : (slot + 1) * BLOCK, :HD]
                acc_v[where] += terms[slot * BLOCK : (slot + 1) * BLOCK, HD:]
        return carry

    lax.fori_loop(0, (2 * places - 1) // unroll, sparse_step, 0)
    for copy in copies[8:]:
        copy.wait()

    copies = [
        pltpu.make_async_copy(acc_k.at[core], own_out.at[0], out_sem.at[0]),
        pltpu.make_async_copy(acc_v.at[core], own_out.at[1], out_sem.at[1]),
    ]
    for copy in copies:
        copy.start()

    def round_other(t, carry):
        where = pl.ds(t * CHUNK, CHUNK)
        mine = acc_k[core, where] * raw_scr[core, where].astype(jnp.float32)
        far = acc_k[1 - core, where]
        theirs = far * raw_scr[1 - core, where].astype(jnp.float32)
        other_out[0, where] = far.astype(jnp.bfloat16)
        other_out[1, where] = acc_v[1 - core, where].astype(jnp.bfloat16)
        return carry + jnp.sum((mine + theirs).reshape(CHUNK * PAIR // 8, 8, HD), axis=0)

    gain_term = lax.fori_loop(0, steps, round_other, jnp.zeros((8, HD), jnp.float32), unroll=2)
    gain_term = jnp.sum(gain_term, axis=0, keepdims=True) * SCALE
    gain_out[...] = jnp.broadcast_to(gain_term, (8, HD))
    for copy in copies:
        copy.wait()


def backward(core, table, own, other, keys, grads, att, weights, dense, places):
    unroll = 9 if (2 * places - 1) % 9 == 0 else 1
    both = (2, places, PAIR, HD)
    half = (places, PAIR, HD)
    blocks = 2 * places
    smem = pl.BlockSpec(memory_space=pltpu.SMEM)
    vmem = pl.BlockSpec(memory_space=pltpu.VMEM)
    hbm = pl.BlockSpec(memory_space=pl.ANY)
    return pl.pallas_call(
        functools.partial(backward_kernel, places, unroll),
        in_specs=[smem, smem] + [hbm] * 7,
        out_specs=[vmem, hbm, vmem, vmem],
        out_shape=[
            jax.ShapeDtypeStruct(half, jnp.bfloat16),
            jax.ShapeDtypeStruct(both, jnp.float32),
            jax.ShapeDtypeStruct(both, jnp.bfloat16),
            jax.ShapeDtypeStruct((8, HD), jnp.float32),
        ],
        scratch_shapes=[
            pltpu.VMEM(both, jnp.bfloat16),
            pltpu.VMEM(both, jnp.bfloat16),
            pltpu.VMEM(half, jnp.bfloat16),
            pltpu.VMEM(half, jnp.bfloat16),
            pltpu.VMEM(half, jnp.bfloat16),
            pltpu.VMEM(weights.shape, jnp.bfloat16),
            pltpu.VMEM(dense.shape, jnp.bfloat16),
            pltpu.VMEM(both, jnp.float32),
            pltpu.VMEM(both, jnp.float32),
            pltpu.VMEM(both, jnp.bfloat16),
            pltpu.SemaphoreType.DMA((10,)),
            pltpu.SemaphoreType.DMA((2,)),
        ],
        compiler_params=pltpu.CompilerParams(vmem_limit_bytes=VMEM_LIMIT),
        cost_estimate=pl.CostEstimate(
            flops=8 * blocks * BLOCK * HD * 3 * NK * BLOCK,
            bytes_accessed=100 << 20,
            transcendentals=0,
        ),
        name="backward",
    )(core, table, own, other, keys, grads, att, weights, dense)


def finish_kernel(own_ref, other_ref, scaled_gain_ref, gain_grad_ref, out_ref):
    gain = scaled_gain_ref[...]
    dkey = own_ref[0] + other_ref[0].astype(jnp.float32)
    out_ref[:, :PAIR] = (dkey * gain).astype(jnp.bfloat16)
    dvalue = own_ref[1] + other_ref[1].astype(jnp.float32)
    out_ref[:, PAIR : 2 * PAIR] = dvalue.astype(jnp.bfloat16)
    total = gain_grad_ref[...]
    high = total.astype(jnp.bfloat16)
    rest = total - high.astype(jnp.float32)
    middle = rest.astype(jnp.bfloat16)
    low = (rest - middle.astype(jnp.float32)).astype(jnp.bfloat16)
    row = lax.broadcasted_iota(jnp.int32, (SPARE, HD), 0)
    spare = jnp.where(
        row == 0,
        high.astype(jnp.float32),
        jnp.where(row == 1, middle.astype(jnp.float32), low.astype(jnp.float32)),
    ).astype(jnp.bfloat16)
    out_ref[:, 2 * PAIR :] = jnp.broadcast_to(spare, (out_ref.shape[0], SPARE, HD))


def finish(own, other, scaled_gain, gain_grad, places):
    group = 8 if places % 8 == 0 else 4
    spec = pl.BlockSpec((2, group, PAIR, HD), lambda i: (0, i, 0, 0))
    row = pl.BlockSpec((1, HD), lambda i: (0, 0))
    rows = 2 * PAIR + SPARE
    return pl.pallas_call(
        finish_kernel,
        grid=(places // group,),
        in_specs=[spec, spec, row, row],
        out_specs=pl.BlockSpec((group, rows, HD), lambda i: (i, 0, 0)),
        out_shape=jax.ShapeDtypeStruct((places, rows, HD), jnp.bfloat16),
        name="finish",
    )(own, other, scaled_gain, gain_grad)


def shards(queries, keys, values, key_gain, random_blocks, out_grad):
    heads = queries.shape[2] // HD
    places = lax.axis_size("seq")
    dp = lax.axis_size("dp")
    core = lax.axis_index("dp") % 2
    cores = core.reshape(1)
    head = lax.axis_index("seq") % heads

    def swap(x, bit=1):
        return lax.ppermute(x, "dp", [(i, i ^ bit) for i in range(dp)])

    def over_seq(x):
        return lax.all_to_all(x, "seq", split_axis=0, concat_axis=0, tiled=True)

    def gather(arrays, spare):
        came = swap(pack(1 - cores, arrays, spare, heads, False))
        both = pack(cores, arrays, spare, heads, True)
        both = lax.dynamic_update_slice(both, came[None], (1 - core, 0, 0, 0))
        return both.reshape(places, both.shape[2], HD)

    def scatter(x, count):
        x = x.reshape(2, heads, x.shape[1], HD)
        came = swap(lax.dynamic_index_in_dim(x, 1 - core, axis=0, keepdims=False))
        return unpack(cores, x, came, count)

    named = random_blocks.reshape(heads, 2, 2, NR).transpose(2, 0, 1, 3).reshape(2, heads, 1, 2 * NR)
    named = jnp.pad(named.astype(jnp.bfloat16), ((0, 0), (0, 0), (0, 0), (0, HD - 2 * NR)))
    gain = lax.dynamic_slice_in_dim(key_gain, head * HD, HD).reshape(1, HD)

    own = over_seq(gather((keys[0], values[0], queries[0]), named))
    grads_in = gather((out_grad[0],), None)
    own, grads_in = lax.optimization_barrier((own, grads_in))
    grads = over_seq(grads_in)
    other = swap(own)
    table = own[:, 3 * PAIR, : 2 * NR].astype(jnp.int32).reshape(2 * places * NR)

    att, weights, dense, keys_scaled = forward(cores, table, gain, own, other, places)
    att_back = over_seq(att)
    dq, part_own, part_other, gain_term = backward(
        cores, table, own, other, keys_scaled, grads, att, weights, dense, places
    )
    att_back, dq = lax.optimization_barrier((att_back, dq))
    dq_back = over_seq(dq)
    part_came = swap(part_other)
    bit = 1
    while bit < dp:
        gain_term = gain_term + swap(gain_term, bit)
        bit *= 2
    dkv = finish(part_own, part_came, gain * SCALE, gain_term[:1], places)
    dq_back, dkv = lax.optimization_barrier((dq_back, dkv))
    dkv_back = over_seq(dkv)
    (attended,) = scatter(att_back, 1)
    (query_grad,) = scatter(dq_back, 1)
    dkv_back, attended, query_grad = lax.optimization_barrier((dkv_back, attended, query_grad))
    key_grad, value_grad = scatter(dkv_back, 2)
    gain_rows = dkv_back[:, 2 * PAIR : 2 * PAIR + 3].astype(jnp.float32)
    gain_grad = jnp.sum(gain_rows.reshape(2, heads, 3, HD), axis=(0, 2)).reshape(heads * HD)
    return (attended[None], query_grad[None], key_grad[None], value_grad[None], gain_grad)


def solution(mesh):
    rows = P("dp", "seq", None)
    return jax.shard_map(
        shards,
        mesh=mesh,
        in_specs=(rows, rows, rows, P(), P(None, "seq", None), rows),
        out_specs=(rows, rows, rows, rows, P()),
        check_vma=False,
    )
```

```python
import functools
import math

import jax
import jax.numpy as jnp
from jax import lax
from jax.experimental import pallas as pl
from jax.experimental.pallas import tpu as pltpu
from jax.sharding import PartitionSpec as P

HD = 128
BLOCK = 64
NR = 3
NK = 8
PAIR = 2 * BLOCK
CHUNK = 4
WIDTH = CHUNK * PAIR
SPARE = 8
NEGATIVE = -1e30
SCALE = HD**-0.5
EXP_SCALE = SCALE * math.log2(math.e)
VMEM_LIMIT = 56 * 1024 * 1024


def nt(a, b):
    return lax.dot_general(a, b, (((1,), (1,)), ((), ())), preferred_element_type=jnp.float32)


def nn(a, b):
    return lax.dot_general(a, b, (((1,), (0,)), ((), ())), preferred_element_type=jnp.float32)


def tn(a, b):
    return lax.dot_general(a, b, (((0,), (0,)), ((), ())), preferred_element_type=jnp.float32)


def pack_kernel(group, count, with_spare, parity_ref, *refs):
    out_ref = refs[-1]
    for h in range(group):
        for slot in range(count):
            for turn in range(2):
                row = slot * PAIR + turn * BLOCK
                out_ref[h, row : row + BLOCK] = refs[2 * slot + turn][:, h * HD : (h + 1) * HD]
        if with_spare:
            out_ref[h, count * PAIR :] = jnp.broadcast_to(
                refs[2 * count][parity_ref[0], h], (SPARE, HD)
            )


def pack(parity, arrays, spare, heads, own):
    group = min(heads, 8)
    count = len(arrays)
    rows = count * PAIR + (SPARE if spare is not None else 0)
    specs = []
    args = []
    for array in arrays:
        for turn in range(2):
            specs.append(
                pl.BlockSpec((BLOCK, group * HD), lambda i, p, turn=turn: (2 * turn + p[0], i))
            )
            args.append(array)
    if spare is not None:
        specs.append(pl.BlockSpec((2, group, 1, HD), lambda i, p: (0, i, 0, 0)))
        args.append(spare)
    if own:
        shape = (2, heads, rows, HD)
        out_spec = pl.BlockSpec((pl.Squeezed(), group, rows, HD), lambda i, p: (p[0], i, 0, 0))
    else:
        shape = (heads, rows, HD)
        out_spec = pl.BlockSpec((group, rows, HD), lambda i, p: (i, 0, 0))
    size = 2 * heads * rows * HD
    return pl.pallas_call(
        functools.partial(pack_kernel, group, count, spare is not None),
        grid_spec=pltpu.PrefetchScalarGridSpec(
            num_scalar_prefetch=1,
            grid=(heads // group,),
            in_specs=specs,
            out_specs=out_spec,
        ),
        out_shape=jax.ShapeDtypeStruct(shape, jnp.bfloat16),
        cost_estimate=pl.CostEstimate(flops=0, bytes_accessed=2 * size, transcendentals=0),
        name="pack_own" if own else "pack_sent",
    )(parity, *args)


def unpack_kernel(group, core_ref, keep_ref, came_ref, *out_refs):
    core = core_ref[0]
    for in_ref, parity in ((keep_ref, core), (came_ref, 1 - core)):
        for h in range(group):
            for slot, ref in enumerate(out_refs):
                for turn in range(2):
                    row = slot * PAIR + turn * BLOCK
                    at = pl.multiple_of((2 * turn + parity) * BLOCK, BLOCK)
                    ref[pl.ds(at, BLOCK), h * HD : (h + 1) * HD] = in_ref[h, row : row + BLOCK]


def unpack(core, keep, came, count):
    heads, rows = keep.shape[1:3]
    group = min(heads, 8)
    return pl.pallas_call(
        functools.partial(unpack_kernel, group),
        grid_spec=pltpu.PrefetchScalarGridSpec(
            num_scalar_prefetch=1,
            grid=(heads // group,),
            in_specs=[
                pl.BlockSpec((pl.Squeezed(), group, rows, HD), lambda i, c: (c[0], i, 0, 0)),
                pl.BlockSpec((group, rows, HD), lambda i, c: (i, 0, 0)),
            ],
            out_specs=[pl.BlockSpec((4 * BLOCK, group * HD), lambda i, c: (0, i))] * count,
        ),
        out_shape=[jax.ShapeDtypeStruct((4 * BLOCK, heads * HD), keep.dtype)] * count,
        cost_estimate=pl.CostEstimate(
            flops=0, bytes_accessed=16 * count * BLOCK * heads * HD, transcendentals=0
        ),
        name="unpack",
    )(core, keep, came)


def locate(block):
    half = block // 2
    return (block % 2, half // 2, pl.ds(pl.multiple_of((half % 2) * BLOCK, BLOCK), BLOCK))


def key_places(table_ref, n, block, total_blocks):
    return [
        (0, 0, pl.ds(0, BLOCK)),
        (1, 0, pl.ds(0, BLOCK)),
        locate(jnp.maximum(block - 1, 0)),
        locate(block),
        locate(jnp.minimum(block + 1, total_blocks - 1)),
    ] + [locate(table_ref[n * NR + r]) for r in range(NR)]


def chunk_rows(ref, t, steps):
    return ref[t // steps, pl.ds((t % steps) * CHUNK, CHUNK)].reshape(WIDTH, HD)


def forward_kernel(
    places,
    unroll,
    core_ref,
    table_ref,
    gain_ref,
    own_ref,
    other_ref,
    att_ref,
    weight_ref,
    dense_ref,
    key_out,
    k_scr,
    v_scr,
    q_scr,
    score_scr,
    weight_scr,
    dense_scr,
    in_sem,
    out_sem,
    weight_sem,
):
    core = core_ref[0]
    total_blocks = 4 * places
    steps = places // CHUNK

    def rows(ref, slot):
        return ref.at[:, slot * PAIR : (slot + 1) * PAIR]

    copies = [
        pltpu.make_async_copy(rows(own_ref, 0), k_scr.at[core], in_sem.at[0]),
        pltpu.make_async_copy(rows(other_ref, 0), k_scr.at[1 - core], in_sem.at[1]),
        pltpu.make_async_copy(rows(own_ref, 2), q_scr, in_sem.at[2]),
        pltpu.make_async_copy(rows(own_ref, 1), v_scr.at[core], in_sem.at[3]),
        pltpu.make_async_copy(rows(other_ref, 1), v_scr.at[1 - core], in_sem.at[4]),
    ]
    for copy in copies:
        copy.start()
    for copy in copies[:3]:
        copy.wait()

    gain = gain_ref[...]
    query = q_scr[0, :BLOCK]

    def lanes(x, op):
        out = x[:, :HD]
        for t in range(1, WIDTH // HD):
            out = op(out, x[:, t * HD : (t + 1) * HD])
        return out

    def dense_scores(t, top):
        where = (t // steps, pl.ds((t % steps) * CHUNK, CHUNK))
        keys = (k_scr[where].astype(jnp.float32) * gain).astype(jnp.bfloat16)
        k_scr[where] = keys
        scores = nt(query, keys.reshape(WIDTH, HD))
        score_scr[t] = scores
        return jnp.maximum(top, lanes(scores, jnp.maximum))

    top = lax.fori_loop(
        0, 2 * steps, dense_scores, jnp.full((BLOCK, HD), NEGATIVE, jnp.float32), unroll=4
    )
    top = jnp.max(top, axis=1, keepdims=True)
    key_copy = pltpu.make_async_copy(k_scr, key_out, out_sem.at[0])
    key_copy.start()
    for copy in copies[3:]:
        copy.wait()

    def dense_expo(t, carry):
        total, numer = carry
        expo = jnp.exp2((score_scr[t] - top) * EXP_SCALE)
        score_scr[t] = expo
        numer = numer + nn(expo.astype(jnp.bfloat16), chunk_rows(v_scr, t, steps))
        return total + lanes(expo, jnp.add), numer

    zero = jnp.zeros((BLOCK, HD), jnp.float32)
    total, numer = lax.fori_loop(0, 2 * steps, dense_expo, (zero, zero), unroll=4)
    inverse = 1.0 / jnp.sum(total, axis=1, keepdims=True)
    att_ref[0, :BLOCK] = (numer * inverse).astype(jnp.bfloat16)

    def dense_weights(t, carry):
        dense_scr[t] = (score_scr[t] * inverse).astype(jnp.bfloat16)
        return carry

    lax.fori_loop(0, 2 * steps, dense_weights, 0, unroll=4)

    dense_copy = pltpu.make_async_copy(dense_scr, dense_ref, out_sem.at[1])
    dense_copy.start()
    column = lax.broadcasted_iota(jnp.int32, (1, NK * BLOCK), 1) // BLOCK

    def sparse_block(n):
        block = 2 * n + core
        listing = key_places(table_ref, n, block, total_blocks)
        key_list = jnp.concatenate([k_scr[where] for where in listing], axis=0)
        value_list = jnp.concatenate([v_scr[where] for where in listing], axis=0)
        mine = (n // 2, pl.ds(pl.multiple_of((n % 2) * BLOCK, BLOCK), BLOCK))
        masked = ((column == 2) & (block == 2)) | ((column == 4) & (block == total_blocks - 1))
        scores = nt(q_scr[mine], key_list) + jnp.where(masked, NEGATIVE, 0.0)
        top = jnp.max(scores, axis=1, keepdims=True)
        expo = jnp.exp2((scores - top) * EXP_SCALE)
        inverse = 1.0 / jnp.sum(expo, axis=1, keepdims=True)
        numer = nn(expo.astype(jnp.bfloat16), value_list)
        return mine, (numer * inverse).astype(jnp.bfloat16), (expo * inverse).astype(jnp.bfloat16)

    def sparse_step(t, carry):
        first = 1 + t * unroll
        done = [sparse_block(first + u) for u in range(unroll)]
        for u, (mine, attended, weights) in enumerate(done):
            att_ref[mine] = attended
            weight_scr[first + u] = weights
        weight_copy(t).start()
        return carry

    def weight_copy(t):
        part = pl.ds(1 + t * unroll, unroll)
        return pltpu.make_async_copy(weight_scr.at[part], weight_ref.at[part], weight_sem.at[t])

    rounds = (2 * places - 1) // unroll
    lax.fori_loop(0, rounds, sparse_step, 0)
    key_copy.wait()
    dense_copy.wait()
    for t in range(rounds):
        weight_copy(t).wait()


def forward(core, table, gain, own, other, places):
    unroll = 9 if (2 * places - 1) % 9 == 0 else 1
    both = (2, places, PAIR, HD)
    smem = pl.BlockSpec(memory_space=pltpu.SMEM)
    vmem = pl.BlockSpec(memory_space=pltpu.VMEM)
    hbm = pl.BlockSpec(memory_space=pl.ANY)
    blocks = 2 * places
    return pl.pallas_call(
        functools.partial(forward_kernel, places, unroll),
        in_specs=[smem, smem, vmem, hbm, hbm],
        out_specs=[vmem, hbm, hbm, hbm],
        out_shape=[
            jax.ShapeDtypeStruct((places, PAIR, HD), jnp.bfloat16),
            jax.ShapeDtypeStruct((blocks, BLOCK, NK * BLOCK), jnp.bfloat16),
            jax.ShapeDtypeStruct((places // 2, BLOCK, WIDTH), jnp.bfloat16),
            jax.ShapeDtypeStruct(both, jnp.bfloat16),
        ],
        scratch_shapes=[
            pltpu.VMEM(both, jnp.bfloat16),
            pltpu.VMEM(both, jnp.bfloat16),
            pltpu.VMEM((places, PAIR, HD), jnp.bfloat16),
            pltpu.VMEM((places // 2, BLOCK, WIDTH), jnp.float32),
            pltpu.VMEM((blocks, BLOCK, NK * BLOCK), jnp.bfloat16),
            pltpu.VMEM((places // 2, BLOCK, WIDTH), jnp.bfloat16),
            pltpu.SemaphoreType.DMA((5,)),
            pltpu.SemaphoreType.DMA((2,)),
            pltpu.SemaphoreType.DMA(((blocks - 1) // unroll,)),
        ],
        compiler_params=pltpu.CompilerParams(vmem_limit_bytes=VMEM_LIMIT),
        cost_estimate=pl.CostEstimate(
            flops=4 * blocks * BLOCK * HD * 3 * NK * BLOCK,
            bytes_accessed=60 << 20,
            transcendentals=blocks * BLOCK * NK * BLOCK,
        ),
        name="forward",
    )(core, table, gain, own, other)


def diagonal(query, grad):
    zero = jnp.zeros_like(query)
    return jnp.concatenate(
        [jnp.concatenate([query, zero], axis=1), jnp.concatenate([zero, grad], axis=1)], axis=0
    )


def joint_terms(dscores, weights, operand):
    return tn(jnp.concatenate([dscores, weights], axis=0), operand)


def backward_kernel(
    places,
    unroll,
    core_ref,
    table_ref,
    own_ref,
    other_ref,
    key_ref,
    grad_ref,
    att_ref,
    weight_ref,
    dense_ref,
    dq_ref,
    own_out,
    other_out,
    gain_out,
    k_scr,
    v_scr,
    q_scr,
    g_scr,
    a_scr,
    weight_scr,
    dense_scr,
    acc_k,
    acc_v,
    raw_scr,
    in_sem,
    out_sem,
):
    core = core_ref[0]
    total_blocks = 4 * places
    steps = places // CHUNK

    def rows(ref, slot):
        return ref.at[:, slot * PAIR : (slot + 1) * PAIR]

    copies = [
        pltpu.make_async_copy(src, dst, in_sem.at[at])
        for at, (src, dst) in enumerate(
            [
                (grad_ref, g_scr),
                (att_ref, a_scr),
                (dense_ref, dense_scr),
                (rows(own_ref, 1), v_scr.at[core]),
                (rows(other_ref, 1), v_scr.at[1 - core]),
                (key_ref, k_scr),
                (rows(own_ref, 2), q_scr),
                (weight_ref, weight_scr),
                (rows(own_ref, 0), raw_scr.at[core]),
                (rows(other_ref, 0), raw_scr.at[1 - core]),
            ]
        )
    ]
    for copy in copies:
        copy.start()
    for copy in copies[:7]:
        copy.wait()

    def row_delta(grad, attended):
        return jnp.sum(
            grad.astype(jnp.float32) * attended.astype(jnp.float32), axis=1, keepdims=True
        )

    query = q_scr[0, :BLOCK]
    grad = g_scr[0, :BLOCK]
    delta = row_delta(grad, a_scr[0, :BLOCK])
    operand = diagonal(query, grad)

    def dense_back(t, dquery):
        weights = dense_scr[t]
        dprobs = nt(grad, chunk_rows(v_scr, t, steps))
        dscores = (weights.astype(jnp.float32) * (dprobs - delta)).astype(jnp.bfloat16)
        where = (t // steps, pl.ds((t % steps) * CHUNK, CHUNK))
        both = joint_terms(dscores, weights, operand)
        acc_k[where] = both[:, :HD].reshape(CHUNK, PAIR, HD)
        acc_v[where] = both[:, HD:].reshape(CHUNK, PAIR, HD)
        return dquery + nn(dscores, chunk_rows(k_scr, t, steps))

    zero = jnp.zeros((BLOCK, HD), jnp.float32)
    dquery = lax.fori_loop(0, 2 * steps, dense_back, zero, unroll=4)
    dq_ref[0, :BLOCK] = (dquery * SCALE).astype(jnp.bfloat16)
    copies[7].wait()

    def sparse_block(n):
        block = 2 * n + core
        listing = key_places(table_ref, n, block, total_blocks)
        key_list = jnp.concatenate([k_scr[where] for where in listing], axis=0)
        value_list = jnp.concatenate([v_scr[where] for where in listing], axis=0)
        mine = (n // 2, pl.ds(pl.multiple_of((n % 2) * BLOCK, BLOCK), BLOCK))
        grad = g_scr[mine]
        weights = weight_scr[n]
        delta = row_delta(grad, a_scr[mine])
        dprobs = nt(grad, value_list)
        dscores = (weights.astype(jnp.float32) * (dprobs - delta)).astype(jnp.bfloat16)
        dquery = nn(dscores, key_list)
        return listing, mine, dquery, joint_terms(dscores, weights, diagonal(q_scr[mine], grad))

    def sparse_step(t, carry):
        done = [sparse_block(1 + t * unroll + u) for u in range(unroll)]
        for listing, mine, dquery, terms in done:
            dq_ref[mine] = (dquery * SCALE).astype(jnp.bfloat16)
            for slot, where in enumerate(listing):
                acc_k[where] += terms[slot * BLOCK : (slot + 1) * BLOCK, :HD]
                acc_v[where] += terms[slot * BLOCK : (slot + 1) * BLOCK, HD:]
        return carry

    lax.fori_loop(0, (2 * places - 1) // unroll, sparse_step, 0)
    for copy in copies[8:]:
        copy.wait()

    copies = [
        pltpu.make_async_copy(acc_k.at[core], own_out.at[0], out_sem.at[0]),
        pltpu.make_async_copy(acc_v.at[core], own_out.at[1], out_sem.at[1]),
    ]
    for copy in copies:
        copy.start()

    def round_other(t, carry):
        where = pl.ds(t * CHUNK, CHUNK)
        mine = acc_k[core, where] * raw_scr[core, where].astype(jnp.float32)
        far = acc_k[1 - core, where]
        theirs = far * raw_scr[1 - core, where].astype(jnp.float32)
        other_out[0, where] = far.astype(jnp.bfloat16)
        other_out[1, where] = acc_v[1 - core, where].astype(jnp.bfloat16)
        return carry + jnp.sum((mine + theirs).reshape(CHUNK * PAIR // 8, 8, HD), axis=0)

    gain_term = lax.fori_loop(0, steps, round_other, jnp.zeros((8, HD), jnp.float32), unroll=2)
    gain_term = jnp.sum(gain_term, axis=0, keepdims=True) * SCALE
    gain_out[...] = jnp.broadcast_to(gain_term, (8, HD))
    for copy in copies:
        copy.wait()


def backward(core, table, own, other, keys, grads, att, weights, dense, places):
    unroll = 9 if (2 * places - 1) % 9 == 0 else 1
    both = (2, places, PAIR, HD)
    half = (places, PAIR, HD)
    blocks = 2 * places
    smem = pl.BlockSpec(memory_space=pltpu.SMEM)
    vmem = pl.BlockSpec(memory_space=pltpu.VMEM)
    hbm = pl.BlockSpec(memory_space=pl.ANY)
    return pl.pallas_call(
        functools.partial(backward_kernel, places, unroll),
        in_specs=[smem, smem] + [hbm] * 7,
        out_specs=[vmem, hbm, vmem, vmem],
        out_shape=[
            jax.ShapeDtypeStruct(half, jnp.bfloat16),
            jax.ShapeDtypeStruct(both, jnp.float32),
            jax.ShapeDtypeStruct(both, jnp.bfloat16),
            jax.ShapeDtypeStruct((8, HD), jnp.float32),
        ],
        scratch_shapes=[
            pltpu.VMEM(both, jnp.bfloat16),
            pltpu.VMEM(both, jnp.bfloat16),
            pltpu.VMEM(half, jnp.bfloat16),
            pltpu.VMEM(half, jnp.bfloat16),
            pltpu.VMEM(half, jnp.bfloat16),
            pltpu.VMEM(weights.shape, jnp.bfloat16),
            pltpu.VMEM(dense.shape, jnp.bfloat16),
            pltpu.VMEM(both, jnp.float32),
            pltpu.VMEM(both, jnp.float32),
            pltpu.VMEM(both, jnp.bfloat16),
            pltpu.SemaphoreType.DMA((10,)),
            pltpu.SemaphoreType.DMA((2,)),
        ],
        compiler_params=pltpu.CompilerParams(vmem_limit_bytes=VMEM_LIMIT),
        cost_estimate=pl.CostEstimate(
            flops=8 * blocks * BLOCK * HD * 3 * NK * BLOCK,
            bytes_accessed=100 << 20,
            transcendentals=0,
        ),
        name="backward",
    )(core, table, own, other, keys, grads, att, weights, dense)


def finish_kernel(own_ref, other_ref, dq_ref, scaled_gain_ref, out_ref):
    gain = scaled_gain_ref[...]
    dkey = own_ref[0] + other_ref[0].astype(jnp.float32)
    out_ref[:, :PAIR] = (dkey * gain).astype(jnp.bfloat16)
    dvalue = own_ref[1] + other_ref[1].astype(jnp.float32)
    out_ref[:, PAIR : 2 * PAIR] = dvalue.astype(jnp.bfloat16)
    out_ref[:, 2 * PAIR : 3 * PAIR] = dq_ref[...]


def finish(own, other, dq, scaled_gain, places):
    group = 8 if places % 8 == 0 else 4
    spec = pl.BlockSpec((2, group, PAIR, HD), lambda i: (0, i, 0, 0))
    rows = 3 * PAIR
    return pl.pallas_call(
        finish_kernel,
        grid=(places // group,),
        in_specs=[
            spec,
            spec,
            pl.BlockSpec((group, PAIR, HD), lambda i: (i, 0, 0)),
            pl.BlockSpec((1, HD), lambda i: (0, 0)),
        ],
        out_specs=pl.BlockSpec((group, rows, HD), lambda i: (i, 0, 0)),
        out_shape=jax.ShapeDtypeStruct((places, rows, HD), jnp.bfloat16),
        cost_estimate=pl.CostEstimate(
            flops=0, bytes_accessed=20 * places * PAIR * HD, transcendentals=0
        ),
        name="finish",
    )(own, other, dq, scaled_gain)


def shards(queries, keys, values, key_gain, random_blocks, out_grad):
    heads = queries.shape[2] // HD
    places = lax.axis_size("seq")
    dp = lax.axis_size("dp")
    core = lax.axis_index("dp") % 2
    cores = core.reshape(1)
    head = lax.axis_index("seq") % heads

    def swap(x, bit=1):
        return lax.ppermute(x, "dp", [(i, i ^ bit) for i in range(dp)])

    def swap_seq(x, bit):
        return lax.ppermute(x, "seq", [(i, i ^ bit) for i in range(places)])

    def over_seq(x):
        return lax.all_to_all(x, "seq", split_axis=0, concat_axis=0, tiled=True)

    def gather(arrays, spare):
        came = swap(pack(1 - cores, arrays, spare, heads, False))
        both = pack(cores, arrays, spare, heads, True)
        both = lax.dynamic_update_slice(both, came[None], (1 - core, 0, 0, 0))
        return both.reshape(places, both.shape[2], HD)

    def scatter(x, count):
        x = x.reshape(2, heads, x.shape[1], HD)
        came = swap(lax.dynamic_index_in_dim(x, 1 - core, axis=0, keepdims=False))
        return unpack(cores, x, came, count)

    named = random_blocks.reshape(heads, 2, 2, NR).transpose(2, 0, 1, 3).reshape(2, heads, 1, 2 * NR)
    named = jnp.pad(named.astype(jnp.bfloat16), ((0, 0), (0, 0), (0, 0), (0, HD - 2 * NR)))
    gain = lax.dynamic_slice_in_dim(key_gain, head * HD, HD).reshape(1, HD)

    own = over_seq(gather((keys[0], values[0], queries[0]), named))
    grads_in = gather((out_grad[0],), None)
    own, grads_in = lax.optimization_barrier((own, grads_in))
    grads = over_seq(grads_in)
    other = swap(own)
    table = own[:, 3 * PAIR, : 2 * NR].astype(jnp.int32).reshape(2 * places * NR)

    att, weights, dense, keys_scaled = forward(cores, table, gain, own, other, places)
    att_back = over_seq(att)
    dq, part_own, part_other, gain_term = backward(
        cores, table, own, other, keys_scaled, grads, att, weights, dense, places
    )
    att_back, part_other = lax.optimization_barrier((att_back, part_other))
    grads_out = finish(part_own, swap(part_other), dq, gain * SCALE, places)
    grads_out, gain_term = lax.optimization_barrier((grads_out, gain_term))
    grads_back = over_seq(grads_out)
    (attended,) = scatter(att_back, 1)
    bit = 1
    while bit < dp:
        gain_term = gain_term + swap(gain_term, bit)
        bit *= 2
    gain_term = gain_term[:1]
    gain_term = gain_term + swap_seq(gain_term, heads)
    bit = 1
    while bit < heads:
        other_heads = swap_seq(gain_term, bit)
        lower = (head // bit) % 2 == 0
        gain_term = jnp.concatenate(
            [
                jnp.where(lower, gain_term, other_heads),
                jnp.where(lower, other_heads, gain_term),
            ],
            axis=0,
        )
        bit *= 2
    gain_grad = gain_term.reshape(heads * HD)
    grads_back, attended, gain_grad = lax.optimization_barrier((grads_back, attended, gain_grad))
    key_grad, value_grad, query_grad = scatter(grads_back, 3)
    return (attended[None], query_grad[None], key_grad[None], value_grad[None], gain_grad)


def solution(mesh):
    rows = P("dp", "seq", None)
    return jax.shard_map(
        shards,
        mesh=mesh,
        in_specs=(rows, rows, rows, P(), P(None, "seq", None), rows),
        out_specs=(rows, rows, rows, rows, P()),
        check_vma=False,
    )
```

```python
import functools
import math

import jax
import jax.numpy as jnp
from jax import lax
from jax.experimental import pallas as pl
from jax.experimental.pallas import tpu as pltpu
from jax.sharding import PartitionSpec as P

HD = 128
BLOCK = 64
NR = 3
NK = 8
PAIR = 2 * BLOCK
CHUNK = 4
WIDTH = CHUNK * PAIR
SPARE = 8
NEGATIVE = -1e30
SCALE = HD**-0.5
EXP_SCALE = SCALE * math.log2(math.e)
VMEM_LIMIT = 56 * 1024 * 1024


def nt(a, b):
    return lax.dot_general(a, b, (((1,), (1,)), ((), ())), preferred_element_type=jnp.float32)


def nn(a, b):
    return lax.dot_general(a, b, (((1,), (0,)), ((), ())), preferred_element_type=jnp.float32)


def tn(a, b):
    return lax.dot_general(a, b, (((0,), (0,)), ((), ())), preferred_element_type=jnp.float32)


def pack_kernel(group, count, with_spare, parity_ref, *refs):
    out_ref = refs[-1]
    for h in range(group):
        for slot in range(count):
            for turn in range(2):
                row = slot * PAIR + turn * BLOCK
                out_ref[h, row : row + BLOCK] = refs[2 * slot + turn][:, h * HD : (h + 1) * HD]
        if with_spare:
            out_ref[h, count * PAIR :] = jnp.broadcast_to(
                refs[2 * count][parity_ref[0], h], (SPARE, HD)
            )


def pack(parity, arrays, spare, heads, own):
    group = min(heads, 8)
    count = len(arrays)
    rows = count * PAIR + (SPARE if spare is not None else 0)
    specs = []
    args = []
    for array in arrays:
        for turn in range(2):
            specs.append(
                pl.BlockSpec((BLOCK, group * HD), lambda i, p, turn=turn: (2 * turn + p[0], i))
            )
            args.append(array)
    if spare is not None:
        specs.append(pl.BlockSpec((2, group, 1, HD), lambda i, p: (0, i, 0, 0)))
        args.append(spare)
    if own:
        shape = (2, heads, rows, HD)
        out_spec = pl.BlockSpec((pl.Squeezed(), group, rows, HD), lambda i, p: (p[0], i, 0, 0))
    else:
        shape = (heads, rows, HD)
        out_spec = pl.BlockSpec((group, rows, HD), lambda i, p: (i, 0, 0))
    size = 2 * heads * rows * HD
    return pl.pallas_call(
        functools.partial(pack_kernel, group, count, spare is not None),
        grid_spec=pltpu.PrefetchScalarGridSpec(
            num_scalar_prefetch=1,
            grid=(heads // group,),
            in_specs=specs,
            out_specs=out_spec,
        ),
        out_shape=jax.ShapeDtypeStruct(shape, jnp.bfloat16),
        cost_estimate=pl.CostEstimate(flops=0, bytes_accessed=2 * size, transcendentals=0),
        name="pack_own" if own else "pack_sent",
    )(parity, *args)


def unpack_kernel(group, core_ref, keep_ref, came_ref, *out_refs):
    core = core_ref[0]
    for in_ref, parity in ((keep_ref, core), (came_ref, 1 - core)):
        for h in range(group):
            for slot, ref in enumerate(out_refs):
                for turn in range(2):
                    row = slot * PAIR + turn * BLOCK
                    at = pl.multiple_of((2 * turn + parity) * BLOCK, BLOCK)
                    ref[pl.ds(at, BLOCK), h * HD : (h + 1) * HD] = in_ref[h, row : row + BLOCK]


def unpack(core, keep, came, count):
    heads, rows = keep.shape[1:3]
    group = min(heads, 8)
    return pl.pallas_call(
        functools.partial(unpack_kernel, group),
        grid_spec=pltpu.PrefetchScalarGridSpec(
            num_scalar_prefetch=1,
            grid=(heads // group,),
            in_specs=[
                pl.BlockSpec((pl.Squeezed(), group, rows, HD), lambda i, c: (c[0], i, 0, 0)),
                pl.BlockSpec((group, rows, HD), lambda i, c: (i, 0, 0)),
            ],
            out_specs=[pl.BlockSpec((4 * BLOCK, group * HD), lambda i, c: (0, i))] * count,
        ),
        out_shape=[jax.ShapeDtypeStruct((4 * BLOCK, heads * HD), keep.dtype)] * count,
        cost_estimate=pl.CostEstimate(
            flops=0, bytes_accessed=16 * count * BLOCK * heads * HD, transcendentals=0
        ),
        name="unpack",
    )(core, keep, came)


def locate(block):
    half = block // 2
    return (block % 2, half // 2, pl.ds(pl.multiple_of((half % 2) * BLOCK, BLOCK), BLOCK))


def key_places(table_ref, n, block, total_blocks):
    return [
        (0, 0, pl.ds(0, BLOCK)),
        (1, 0, pl.ds(0, BLOCK)),
        locate(jnp.maximum(block - 1, 0)),
        locate(block),
        locate(jnp.minimum(block + 1, total_blocks - 1)),
    ] + [locate(table_ref[n * NR + r]) for r in range(NR)]


def chunk_rows(ref, t, steps):
    return ref[t // steps, pl.ds((t % steps) * CHUNK, CHUNK)].reshape(WIDTH, HD)


def forward_kernel(
    places,
    unroll,
    core_ref,
    table_ref,
    gain_ref,
    own_ref,
    other_ref,
    att_ref,
    weight_ref,
    dense_ref,
    key_out,
    k_scr,
    v_scr,
    q_scr,
    score_scr,
    weight_scr,
    dense_scr,
    in_sem,
    out_sem,
    weight_sem,
):
    core = core_ref[0]
    total_blocks = 4 * places
    steps = places // CHUNK

    def rows(ref, slot):
        return ref.at[:, slot * PAIR : (slot + 1) * PAIR]

    copies = [
        pltpu.make_async_copy(rows(own_ref, 0), k_scr.at[core], in_sem.at[0]),
        pltpu.make_async_copy(rows(other_ref, 0), k_scr.at[1 - core], in_sem.at[1]),
        pltpu.make_async_copy(rows(own_ref, 2), q_scr, in_sem.at[2]),
        pltpu.make_async_copy(rows(own_ref, 1), v_scr.at[core], in_sem.at[3]),
        pltpu.make_async_copy(rows(other_ref, 1), v_scr.at[1 - core], in_sem.at[4]),
    ]
    for copy in copies:
        copy.start()
    for copy in copies[:3]:
        copy.wait()

    gain = gain_ref[...]
    query = q_scr[0, :BLOCK]

    def lanes(x, op):
        out = x[:, :HD]
        for t in range(1, WIDTH // HD):
            out = op(out, x[:, t * HD : (t + 1) * HD])
        return out

    def dense_scores(t, top):
        where = (t // steps, pl.ds((t % steps) * CHUNK, CHUNK))
        keys = (k_scr[where].astype(jnp.float32) * gain).astype(jnp.bfloat16)
        k_scr[where] = keys
        scores = nt(query, keys.reshape(WIDTH, HD))
        score_scr[t] = scores
        return jnp.maximum(top, lanes(scores, jnp.maximum))

    top = lax.fori_loop(
        0, 2 * steps, dense_scores, jnp.full((BLOCK, HD), NEGATIVE, jnp.float32), unroll=4
    )
    top = jnp.max(top, axis=1, keepdims=True)
    key_copy = pltpu.make_async_copy(k_scr, key_out, out_sem.at[0])
    key_copy.start()
    for copy in copies[3:]:
        copy.wait()

    def dense_expo(t, carry):
        total, numer = carry
        expo = jnp.exp2((score_scr[t] - top) * EXP_SCALE)
        score_scr[t] = expo
        numer = numer + nn(expo.astype(jnp.bfloat16), chunk_rows(v_scr, t, steps))
        return total + lanes(expo, jnp.add), numer

    zero = jnp.zeros((BLOCK, HD), jnp.float32)
    total, numer = lax.fori_loop(0, 2 * steps, dense_expo, (zero, zero), unroll=4)
    inverse = 1.0 / jnp.sum(total, axis=1, keepdims=True)
    att_ref[0, :BLOCK] = (numer * inverse).astype(jnp.bfloat16)

    def dense_weights(t, carry):
        dense_scr[t] = (score_scr[t] * inverse).astype(jnp.bfloat16)
        return carry

    lax.fori_loop(0, 2 * steps, dense_weights, 0, unroll=4)

    dense_copy = pltpu.make_async_copy(dense_scr, dense_ref, out_sem.at[1])
    dense_copy.start()
    column = lax.broadcasted_iota(jnp.int32, (1, NK * BLOCK), 1) // BLOCK

    def sparse_block(n):
        block = 2 * n + core
        listing = key_places(table_ref, n, block, total_blocks)
        key_list = jnp.concatenate([k_scr[where] for where in listing], axis=0)
        value_list = jnp.concatenate([v_scr[where] for where in listing], axis=0)
        mine = (n // 2, pl.ds(pl.multiple_of((n % 2) * BLOCK, BLOCK), BLOCK))
        masked = ((column == 2) & (block == 2)) | ((column == 4) & (block == total_blocks - 1))
        scores = nt(q_scr[mine], key_list) + jnp.where(masked, NEGATIVE, 0.0)
        top = jnp.max(scores, axis=1, keepdims=True)
        expo = jnp.exp2((scores - top) * EXP_SCALE)
        inverse = 1.0 / jnp.sum(expo, axis=1, keepdims=True)
        numer = nn(expo.astype(jnp.bfloat16), value_list)
        return mine, (numer * inverse).astype(jnp.bfloat16), (expo * inverse).astype(jnp.bfloat16)

    def sparse_step(t, carry):
        first = 1 + t * unroll
        done = [sparse_block(first + u) for u in range(unroll)]
        for u, (mine, attended, weights) in enumerate(done):
            att_ref[mine] = attended
            weight_scr[first + u] = weights
        weight_copy(t).start()
        return carry

    def weight_copy(t):
        part = pl.ds(1 + t * unroll, unroll)
        return pltpu.make_async_copy(weight_scr.at[part], weight_ref.at[part], weight_sem.at[t])

    rounds = (2 * places - 1) // unroll
    lax.fori_loop(0, rounds, sparse_step, 0)
    key_copy.wait()
    dense_copy.wait()
    for t in range(rounds):
        weight_copy(t).wait()


def forward(core, table, gain, own, other, places):
    unroll = 9 if (2 * places - 1) % 9 == 0 else 1
    both = (2, places, PAIR, HD)
    smem = pl.BlockSpec(memory_space=pltpu.SMEM)
    vmem = pl.BlockSpec(memory_space=pltpu.VMEM)
    hbm = pl.BlockSpec(memory_space=pl.ANY)
    blocks = 2 * places
    return pl.pallas_call(
        functools.partial(forward_kernel, places, unroll),
        in_specs=[smem, smem, vmem, hbm, hbm],
        out_specs=[vmem, hbm, hbm, hbm],
        out_shape=[
            jax.ShapeDtypeStruct((places, PAIR, HD), jnp.bfloat16),
            jax.ShapeDtypeStruct((blocks, BLOCK, NK * BLOCK), jnp.bfloat16),
            jax.ShapeDtypeStruct((places // 2, BLOCK, WIDTH), jnp.bfloat16),
            jax.ShapeDtypeStruct(both, jnp.bfloat16),
        ],
        scratch_shapes=[
            pltpu.VMEM(both, jnp.bfloat16),
            pltpu.VMEM(both, jnp.bfloat16),
            pltpu.VMEM((places, PAIR, HD), jnp.bfloat16),
            pltpu.VMEM((places // 2, BLOCK, WIDTH), jnp.float32),
            pltpu.VMEM((blocks, BLOCK, NK * BLOCK), jnp.bfloat16),
            pltpu.VMEM((places // 2, BLOCK, WIDTH), jnp.bfloat16),
            pltpu.SemaphoreType.DMA((5,)),
            pltpu.SemaphoreType.DMA((2,)),
            pltpu.SemaphoreType.DMA(((blocks - 1) // unroll,)),
        ],
        compiler_params=pltpu.CompilerParams(vmem_limit_bytes=VMEM_LIMIT),
        cost_estimate=pl.CostEstimate(
            flops=4 * blocks * BLOCK * HD * 3 * NK * BLOCK,
            bytes_accessed=60 << 20,
            transcendentals=blocks * BLOCK * NK * BLOCK,
        ),
        name="forward",
    )(core, table, gain, own, other)


def diagonal(query, grad):
    zero = jnp.zeros_like(query)
    return jnp.concatenate(
        [jnp.concatenate([query, zero], axis=1), jnp.concatenate([zero, grad], axis=1)], axis=0
    )


def joint_terms(dscores, weights, operand):
    return tn(jnp.concatenate([dscores, weights], axis=0), operand)


def backward_kernel(
    places,
    unroll,
    core_ref,
    table_ref,
    own_ref,
    other_ref,
    key_ref,
    grad_ref,
    att_ref,
    weight_ref,
    dense_ref,
    dq_ref,
    own_out,
    other_out,
    gain_out,
    k_scr,
    v_scr,
    q_scr,
    g_scr,
    a_scr,
    weight_scr,
    dense_scr,
    acc_k,
    acc_v,
    raw_scr,
    first_scr,
    in_sem,
    out_sem,
):
    core = core_ref[0]
    total_blocks = 4 * places
    steps = places // CHUNK

    def rows(ref, slot):
        return ref.at[:, slot * PAIR : (slot + 1) * PAIR]

    copies = [
        pltpu.make_async_copy(src, dst, in_sem.at[at])
        for at, (src, dst) in enumerate(
            [
                (own_ref.at[0, 2 * PAIR : 2 * PAIR + BLOCK], first_scr.at[0]),
                (grad_ref.at[0, :BLOCK], first_scr.at[1]),
                (att_ref.at[0, :BLOCK], first_scr.at[2]),
                (dense_ref, dense_scr),
                (rows(own_ref, 1), v_scr.at[core]),
                (rows(other_ref, 1), v_scr.at[1 - core]),
                (key_ref, k_scr),
                (grad_ref, g_scr),
                (att_ref, a_scr),
                (rows(own_ref, 2), q_scr),
                (weight_ref, weight_scr),
                (rows(own_ref, 0), raw_scr.at[core]),
                (rows(other_ref, 0), raw_scr.at[1 - core]),
            ]
        )
    ]
    for copy in copies:
        copy.start()
    for copy in copies[:7]:
        copy.wait()

    def row_delta(grad, attended):
        return jnp.sum(
            grad.astype(jnp.float32) * attended.astype(jnp.float32), axis=1, keepdims=True
        )

    query = first_scr[0]
    grad = first_scr[1]
    delta = row_delta(grad, first_scr[2])
    operand = diagonal(query, grad)

    def dense_back(t, dquery):
        weights = dense_scr[t]
        dprobs = nt(grad, chunk_rows(v_scr, t, steps))
        dscores = (weights.astype(jnp.float32) * (dprobs - delta)).astype(jnp.bfloat16)
        where = (t // steps, pl.ds((t % steps) * CHUNK, CHUNK))
        both = joint_terms(dscores, weights, operand)
        acc_k[where] = both[:, :HD].reshape(CHUNK, PAIR, HD)
        acc_v[where] = both[:, HD:].reshape(CHUNK, PAIR, HD)
        return dquery + nn(dscores, chunk_rows(k_scr, t, steps))

    zero = jnp.zeros((BLOCK, HD), jnp.float32)
    dquery = lax.fori_loop(0, 2 * steps, dense_back, zero, unroll=4)
    dq_ref[0, :BLOCK] = (dquery * SCALE).astype(jnp.bfloat16)
    for copy in copies[7:11]:
        copy.wait()

    def sparse_block(n):
        block = 2 * n + core
        listing = key_places(table_ref, n, block, total_blocks)
        key_list = jnp.concatenate([k_scr[where] for where in listing], axis=0)
        value_list = jnp.concatenate([v_scr[where] for where in listing], axis=0)
        mine = (n // 2, pl.ds(pl.multiple_of((n % 2) * BLOCK, BLOCK), BLOCK))
        grad = g_scr[mine]
        weights = weight_scr[n]
        delta = row_delta(grad, a_scr[mine])
        dprobs = nt(grad, value_list)
        dscores = (weights.astype(jnp.float32) * (dprobs - delta)).astype(jnp.bfloat16)
        dquery = nn(dscores, key_list)
        return listing, mine, dquery, joint_terms(dscores, weights, diagonal(q_scr[mine], grad))

    def sparse_step(t, carry):
        done = [sparse_block(1 + t * unroll + u) for u in range(unroll)]
        for listing, mine, dquery, terms in done:
            dq_ref[mine] = (dquery * SCALE).astype(jnp.bfloat16)
            for slot, where in enumerate(listing):
                acc_k[where] += terms[slot * BLOCK : (slot + 1) * BLOCK, :HD]
                acc_v[where] += terms[slot * BLOCK : (slot + 1) * BLOCK, HD:]
        return carry

    lax.fori_loop(0, (2 * places - 1) // unroll, sparse_step, 0)
    for copy in copies[11:]:
        copy.wait()

    copies = [
        pltpu.make_async_copy(acc_k.at[core], own_out.at[0], out_sem.at[0]),
        pltpu.make_async_copy(acc_v.at[core], own_out.at[1], out_sem.at[1]),
    ]
    for copy in copies:
        copy.start()

    def round_other(t, carry):
        where = pl.ds(t * CHUNK, CHUNK)
        mine = acc_k[core, where] * raw_scr[core, where].astype(jnp.float32)
        far = acc_k[1 - core, where]
        theirs = far * raw_scr[1 - core, where].astype(jnp.float32)
        other_out[0, where] = far.astype(jnp.bfloat16)
        other_out[1, where] = acc_v[1 - core, where].astype(jnp.bfloat16)
        return carry + jnp.sum((mine + theirs).reshape(CHUNK * PAIR // 8, 8, HD), axis=0)

    gain_term = lax.fori_loop(0, steps, round_other, jnp.zeros((8, HD), jnp.float32), unroll=2)
    gain_term = jnp.sum(gain_term, axis=0, keepdims=True) * SCALE
    gain_out[...] = jnp.broadcast_to(gain_term, (8, HD))
    for copy in copies:
        copy.wait()


def backward(core, table, own, other, keys, grads, att, weights, dense, places):
    unroll = 9 if (2 * places - 1) % 9 == 0 else 1
    both = (2, places, PAIR, HD)
    half = (places, PAIR, HD)
    blocks = 2 * places
    smem = pl.BlockSpec(memory_space=pltpu.SMEM)
    vmem = pl.BlockSpec(memory_space=pltpu.VMEM)
    hbm = pl.BlockSpec(memory_space=pl.ANY)
    return pl.pallas_call(
        functools.partial(backward_kernel, places, unroll),
        in_specs=[smem, smem] + [hbm] * 7,
        out_specs=[vmem, hbm, vmem, vmem],
        out_shape=[
            jax.ShapeDtypeStruct(half, jnp.bfloat16),
            jax.ShapeDtypeStruct(both, jnp.float32),
            jax.ShapeDtypeStruct(both, jnp.bfloat16),
            jax.ShapeDtypeStruct((8, HD), jnp.float32),
        ],
        scratch_shapes=[
            pltpu.VMEM(both, jnp.bfloat16),
            pltpu.VMEM(both, jnp.bfloat16),
            pltpu.VMEM(half, jnp.bfloat16),
            pltpu.VMEM(half, jnp.bfloat16),
            pltpu.VMEM(half, jnp.bfloat16),
            pltpu.VMEM(weights.shape, jnp.bfloat16),
            pltpu.VMEM(dense.shape, jnp.bfloat16),
            pltpu.VMEM(both, jnp.float32),
            pltpu.VMEM(both, jnp.float32),
            pltpu.VMEM(both, jnp.bfloat16),
            pltpu.VMEM((3, BLOCK, HD), jnp.bfloat16),
            pltpu.SemaphoreType.DMA((13,)),
            pltpu.SemaphoreType.DMA((2,)),
        ],
        compiler_params=pltpu.CompilerParams(vmem_limit_bytes=VMEM_LIMIT),
        cost_estimate=pl.CostEstimate(
            flops=8 * blocks * BLOCK * HD * 3 * NK * BLOCK,
            bytes_accessed=100 << 20,
            transcendentals=0,
        ),
        name="backward",
    )(core, table, own, other, keys, grads, att, weights, dense)


def finish_kernel(own_ref, other_ref, scaled_gain_ref, gain_grad_ref, out_ref):
    gain = scaled_gain_ref[...]
    dkey = own_ref[0] + other_ref[0].astype(jnp.float32)
    out_ref[:, :PAIR] = (dkey * gain).astype(jnp.bfloat16)
    dvalue = own_ref[1] + other_ref[1].astype(jnp.float32)
    out_ref[:, PAIR : 2 * PAIR] = dvalue.astype(jnp.bfloat16)
    total = gain_grad_ref[...]
    high = total.astype(jnp.bfloat16)
    rest = total - high.astype(jnp.float32)
    middle = rest.astype(jnp.bfloat16)
    low = (rest - middle.astype(jnp.float32)).astype(jnp.bfloat16)
    row = lax.broadcasted_iota(jnp.int32, (SPARE, HD), 0)
    spare = jnp.where(
        row == 0,
        high.astype(jnp.float32),
        jnp.where(row == 1, middle.astype(jnp.float32), low.astype(jnp.float32)),
    ).astype(jnp.bfloat16)
    out_ref[:, 2 * PAIR :] = jnp.broadcast_to(spare, (out_ref.shape[0], SPARE, HD))


def finish(own, other, scaled_gain, gain_grad, places):
    group = 8 if places % 8 == 0 else 4
    spec = pl.BlockSpec((2, group, PAIR, HD), lambda i: (0, i, 0, 0))
    row = pl.BlockSpec((1, HD), lambda i: (0, 0))
    rows = 2 * PAIR + SPARE
    return pl.pallas_call(
        finish_kernel,
        grid=(places // group,),
        in_specs=[spec, spec, row, row],
        out_specs=pl.BlockSpec((group, rows, HD), lambda i: (i, 0, 0)),
        out_shape=jax.ShapeDtypeStruct((places, rows, HD), jnp.bfloat16),
        name="finish",
    )(own, other, scaled_gain, gain_grad)


def shards(queries, keys, values, key_gain, random_blocks, out_grad):
    heads = queries.shape[2] // HD
    places = lax.axis_size("seq")
    dp = lax.axis_size("dp")
    core = lax.axis_index("dp") % 2
    cores = core.reshape(1)
    head = lax.axis_index("seq") % heads

    def swap(x, bit=1):
        return lax.ppermute(x, "dp", [(i, i ^ bit) for i in range(dp)])

    def over_seq(x):
        return lax.all_to_all(x, "seq", split_axis=0, concat_axis=0, tiled=True)

    def gather(arrays, spare):
        came = swap(pack(1 - cores, arrays, spare, heads, False))
        both = pack(cores, arrays, spare, heads, True)
        both = lax.dynamic_update_slice(both, came[None], (1 - core, 0, 0, 0))
        return both.reshape(places, both.shape[2], HD)

    def scatter(x, count):
        x = x.reshape(2, heads, x.shape[1], HD)
        came = swap(lax.dynamic_index_in_dim(x, 1 - core, axis=0, keepdims=False))
        return unpack(cores, x, came, count)

    named = random_blocks.reshape(heads, 2, 2, NR).transpose(2, 0, 1, 3).reshape(2, heads, 1, 2 * NR)
    named = jnp.pad(named.astype(jnp.bfloat16), ((0, 0), (0, 0), (0, 0), (0, HD - 2 * NR)))
    gain = lax.dynamic_slice_in_dim(key_gain, head * HD, HD).reshape(1, HD)

    own = over_seq(gather((keys[0], values[0], queries[0]), named))
    grads_in = gather((out_grad[0],), None)
    own, grads_in = lax.optimization_barrier((own, grads_in))
    grads = over_seq(grads_in)
    other = swap(own)
    table = own[:, 3 * PAIR, : 2 * NR].astype(jnp.int32).reshape(2 * places * NR)

    att, weights, dense, keys_scaled = forward(cores, table, gain, own, other, places)
    att_back = over_seq(att)
    dq, part_own, part_other, gain_term = backward(
        cores, table, own, other, keys_scaled, grads, att, weights, dense, places
    )
    att_back, dq = lax.optimization_barrier((att_back, dq))
    dq_back = over_seq(dq)
    part_came = swap(part_other)
    bit = 1
    while bit < dp:
        gain_term = gain_term + swap(gain_term, bit)
        bit *= 2
    dkv = finish(part_own, part_came, gain * SCALE, gain_term[:1], places)
    dq_back, dkv = lax.optimization_barrier((dq_back, dkv))
    dkv_back = over_seq(dkv)
    (attended,) = scatter(att_back, 1)
    (query_grad,) = scatter(dq_back, 1)
    dkv_back, attended, query_grad = lax.optimization_barrier((dkv_back, attended, query_grad))
    key_grad, value_grad = scatter(dkv_back, 2)
    gain_rows = dkv_back[:, 2 * PAIR : 2 * PAIR + 3].astype(jnp.float32)
    gain_grad = jnp.sum(gain_rows.reshape(2, heads, 3, HD), axis=(0, 2)).reshape(heads * HD)
    return (attended[None], query_grad[None], key_grad[None], value_grad[None], gain_grad)


def solution(mesh):
    rows = P("dp", "seq", None)
    return jax.shard_map(
        shards,
        mesh=mesh,
        in_specs=(rows, rows, rows, P(), P(None, "seq", None), rows),
        out_specs=(rows, rows, rows, rows, P()),
        check_vma=False,
    )
```
